32 devices in a mesh: ga: 2 (over y), gx: 16 (over z, x, core).
Axes of the slice: x: 2, y: 2, z: 4, core: 2. Of those that a mesh axis runs over, the one named last changes fastest.
Arguments:
- fields: bfloat16 [2048, 512, 128], P('gx', 'ga'), parts along dimension 1, may hold values from -6 to 6
- cotangent: bfloat16 [2048, 512, 128], P('gx', 'ga'), parts along dimension 1, may hold values from -6 to 6
- point_weight: bfloat16 [128, 128], replicated, may hold values from -0.5 to 0.5
- mix_weight: bfloat16 [12, 128, 128], replicated, may hold values from -0.5 to 0.5
- bias_vec: bfloat16 [128], replicated, may hold values from -3 to 3
Outputs:
- grad_input: bfloat16 [2048, 512, 128], P('gx', 'ga'), parts along dimension 1
- grad_mix: bfloat16 [24, 128, 128], P('ga'), parts along dimension 0
- grad_point: bfloat16 [256, 128], P('ga'), parts along dimension 0
- grad_bias: bfloat16 [256], P('ga'), parts along dimension 0
The draws below stay inside these ranges and needn't reach their ends.
There are 2 independent parts, one for each index of `ga`. The reference program is written for one: setup_inputs(seed, part) draws one part's arguments, and reference() takes and returns one part's arrays. A program takes and returns all parts, laid end to end along the dimension named above; an argument that names none is the same for every part. Nothing has to cross between parts.
All inputs are finite; a program needn't handle non-finite values.
Results may differ from the reference program's by a relative error of at most 0.012.
Values sent between devices are 32-bit elements; how exact they have to be, the bound alone decides.
A program may use at most 128 MiB of HBM per device.

```python
import math
import jax
import jax.numpy as jnp
import numpy as np
from jax import lax

NX = 2048
C = 128
LEVELS = 11
NY = 256


def block_scale(key, extent, pieces, smallest, top_value):
    level, own = 1.0, jax.random.fold_in(key, 6)
    for position, shards_of in pieces:
        heights = jnp.exp(jax.random.uniform(jax.random.fold_in(own, position), (shards_of,), jnp.float32, smallest / len(pieces), top_value / len(pieces)))
        level = level * jnp.repeat(heights, extent[position] // shards_of).reshape([-1 if axis == position else 1 for axis in range(len(extent))])
    return level


def noise(key, shape, spread, most, split=(), held_as=jnp.bfloat16):
    values = jax.random.normal(key, shape, jnp.float32) * spread
    if len(split) > 0:
        values = block_scale(key, shape, split, -0.22, 0.18) * values
    return jnp.clip(values, min=-most, max=most).astype(held_as)


def setup_inputs(seed: int = 0, part: int = 0) -> dict:
    keys = jax.random.split(jax.random.key(seed), 6)
    part_keys = jax.random.split(jax.random.fold_in(keys[5], part), 6)
    fields = noise(part_keys[0], (NX, NY, C), 1.0, 6.0, ((0, 16),))
    cotangent = noise(part_keys[1], (NX, NY, C), 1.0, 6.0, ((0, 16),))
    point_weight = noise(keys[2], (C, C), C ** -0.5, 0.5)
    mix_weight = noise(keys[3], (LEVELS + 1, C, C), C ** -0.5, 0.5)
    bias_vec = noise(keys[4], (C,), 0.5, 3.0)
    return dict(fields=fields, cotangent=cotangent, point_weight=point_weight, mix_weight=mix_weight, bias_vec=bias_vec)


root_half = 0.7071067811865476

def haar_forward(signal, depth_count):
    for degree in range(depth_count):
        stride = 2 ** degree
        shaped = signal.reshape((signal.shape[0] // (2 * stride), 2, stride) + signal.shape[1:])
        even_rows = shaped[:, 0, 0]
        odd_rows = shaped[:, 1, 0]
        shaped = shaped.at[:, 0, 0].set((even_rows + odd_rows) * root_half)
        shaped = shaped.at[:, 1, 0].set((odd_rows - even_rows) * root_half)
        signal = shaped.reshape(signal.shape)
    return signal

def haar_inverse(signal, depth_count):
    for degree in reversed(range(depth_count)):
        stride = 2 ** degree
        shaped = signal.reshape((signal.shape[0] // (2 * stride), 2, stride) + signal.shape[1:])
        coarse_rows = shaped[:, 0, 0]
        detail_rows = shaped[:, 1, 0]
        shaped = shaped.at[:, 0, 0].set((coarse_rows - detail_rows) * root_half)
        shaped = shaped.at[:, 1, 0].set((coarse_rows + detail_rows) * root_half)
        signal = shaped.reshape(signal.shape)
    return signal

def mix_levels(coeffs_b, weights, depth_count, first_weight):
    output = jnp.zeros(coeffs_b.shape, jnp.float32)
    for degree in range(depth_count):
        stride = 2 ** degree
        picked = coeffs_b[stride::2 * stride]
        output = output.at[stride::2 * stride].set(jnp.dot(picked, weights[degree], preferred_element_type=jnp.float32))
    output = output.at[0].set(jnp.dot(coeffs_b[0], first_weight, preferred_element_type=jnp.float32))
    return output

def outer_sum(left, right):
    left_flat = left.reshape((-1, left.shape[-1]))
    right_flat = right.reshape((-1, right.shape[-1]))
    return lax.dot_general(left_flat, right_flat, (((0,), (0,)), ((), ())), preferred_element_type=jnp.float32)

def gelu_slope(pre_act, cotangent):
    unused_out, pullback = jax.vjp(jax.nn.gelu, pre_act)
    return pullback(cotangent.astype(pre_act.dtype))[0].astype(jnp.bfloat16)

def level_factors(columns):
    counts = [columns * NX / 2 ** (degree + 1) for degree in range(LEVELS)] + [columns]
    return np.array([1.0 / math.sqrt(value) for value in counts], np.float32)

def reference(fields, cotangent, point_weight, mix_weight, bias_vec):
    coeffs = haar_forward(fields.astype(jnp.float32), LEVELS)
    coeffs_b = coeffs.astype(jnp.bfloat16)
    mixed_rows = mix_levels(coeffs_b, mix_weight, LEVELS, mix_weight[LEVELS])
    spectral = haar_inverse(mixed_rows, LEVELS)
    pre_act = spectral + jnp.dot(fields, point_weight, preferred_element_type=jnp.float32) + bias_vec.astype(jnp.float32)
    slope_b = gelu_slope(pre_act, cotangent)
    back_coeffs = haar_forward(slope_b.astype(jnp.float32), LEVELS)
    back_b = back_coeffs.astype(jnp.bfloat16)
    grads_list = []
    for degree in range(LEVELS):
        stride = 2 ** degree
        grads_list.append(outer_sum(coeffs_b[stride::2 * stride], back_b[stride::2 * stride]))
    grads_list.append(outer_sum(coeffs_b[0:1], back_b[0:1]))
    factors = jnp.asarray(level_factors(fields.shape[1]))
    grad_mix = (jnp.stack(grads_list) * factors[:, None, None]).astype(jnp.bfloat16)
    scale_all = 1.0 / math.sqrt(NX * fields.shape[1])
    grad_point = (outer_sum(fields, slope_b) * scale_all).astype(jnp.bfloat16)
    grad_bias = (lax.optimization_barrier(jnp.sum(slope_b.astype(jnp.float32), axis=(0, 1))) * scale_all).astype(jnp.bfloat16)
    transposed = jnp.swapaxes(mix_weight, 1, 2)
    back_mixed = mix_levels(back_b, transposed, LEVELS, transposed[LEVELS])
    grad_input = (haar_inverse(back_mixed, LEVELS) + jnp.dot(slope_b, point_weight.T, preferred_element_type=jnp.float32)).astype(jnp.bfloat16)
    return (grad_input, grad_mix, grad_point, grad_bias)
```

```python
import functools
import math

import jax
import jax.numpy as jnp
from jax import lax
from jax.experimental import pallas as pl
from jax.experimental.pallas import tpu as pltpu
from jax.sharding import PartitionSpec as P

F32 = jnp.float32
BF16 = jnp.bfloat16
LANES = 16
GELU_K = math.sqrt(2.0 / math.pi)
GELU_C = 0.044715
GELU_A = (GELU_K * GELU_C) ** (1.0 / 3.0)
GELU_B = GELU_K / GELU_A


def offset(rows, level):
    return rows - (rows >> level)


def outer(left, right):
    return lax.dot_general(left, right, (((0,), (0,)), ((), ())), preferred_element_type=F32)


def apply_weight(rows, weight, turned):
    sides = (((1,), (1 if turned else 0,)), ((), ()))
    return lax.dot_general(rows, weight, sides, preferred_element_type=F32)


def slope_of(value, cot):
    square = value * value
    bend = jnp.tanh(value * (GELU_B + square))
    ramp = value * (0.5 * GELU_B + 1.5 * square)
    return cot * ((1.0 + bend) * (0.5 + (1.0 - bend) * ramp))


def join_weights(mix_ref, point_ref, scales, factor, joined):
    point = point_ref[...].astype(F32)
    for level, scale in enumerate(scales):
        joined[level] = ((mix_ref[level].astype(F32) + point) * (scale * factor)).astype(BF16)


def mix_block(depth, coeff_ref, weight_ref, mixed_ref, turned):
    rows = 1 << depth
    wide = coeff_ref.shape[1]
    for level in range(depth):
        first, count = offset(rows, level), rows >> (level + 1)
        flat = coeff_ref[first : first + count].reshape(count * wide, coeff_ref.shape[2])
        mixed_ref[first : first + count] = (
            apply_weight(flat, weight_ref[level], turned)
            .reshape(count, wide, weight_ref.shape[2])
            .astype(mixed_ref.dtype)
        )


class Stream:
    def __init__(self, total, slots, result, send, recv, base, length, digits, me):
        self.total, self.slots, self.result = total, slots, result
        self.send, self.recv = send, recv
        start, place, sem = base, 0, 0
        scatter = []
        for stride, radix in digits:
            mine = lax.rem(me // stride, radix)
            split = length % radix == 0
            size = length // radix if split else length
            keep = start + mine * size if split else start
            plan = []
            for turn in range(1, radix):
                other = lax.rem(mine + turn, radix)
                give = start + other * size if split else start
                plan.append((me + (other - mine) * stride, give, place + (turn - 1) * size, sem + turn - 1))
            scatter.append(("sum", plan, split, size, keep))
            start, length = keep, size
            place, sem = place + (radix - 1) * size, sem + radix - 1
        self.stages = scatter[:]
        for kind, plan, split, size, keep in scatter[::-1]:
            if split:
                again = [(peer, keep, keep, sem + turn) for turn, (peer, _, _, _) in enumerate(plan)]
                self.stages.append(("spread", again, split, size, keep))
                sem += len(plan)
        self.last = len(scatter) - 1

    def copies(self, index):
        kind, plan, split, size, keep = self.stages[index]
        source = self.total if kind == "sum" else self.result
        target = self.slots if kind == "sum" else self.result
        return [
            pltpu.make_async_remote_copy(
                src_ref=source.at[pl.ds(give, size)],
                dst_ref=target.at[pl.ds(place, size)],
                send_sem=self.send.at[sem],
                recv_sem=self.recv.at[sem],
                device_id={"gx": peer},
                device_id_type=pl.DeviceIdType.MESH,
            )
            for peer, give, place, sem in plan
        ]

    def start(self, index):
        if index < len(self.stages):
            for copy in self.copies(index):
                copy.start()

    def finish(self, index):
        if index >= len(self.stages):
            return
        for copy in self.copies(index):
            copy.wait()
        kind, plan, split, size, keep = self.stages[index]
        if kind == "sum":
            here = pl.ds(keep, size)
            into = self.result if index == self.last else self.total
            value = self.total[here]
            for _, _, place, _ in plan:
                value = value + self.slots[pl.ds(place, size)]
            into[here] = value


def stream_needs(length, digits):
    place, sem = 0, 0
    for stride, radix in digits:
        split = length % radix == 0
        size = length // radix if split else length
        place, sem = place + (radix - 1) * size, sem + (radix - 1) * (2 if split else 1)
        length = size
    return place, sem


def digit_orders(count):
    bits = count.bit_length() - 2
    plan, stride = [(1, 2)], 2
    while bits > 0:
        size = 1 if bits % 2 else 2
        plan.append((stride, 1 << size))
        stride, bits = stride << size, bits - size
    return plan, plan[:1] + plan[2:] + plan[1:2]


def far_levels(count, first_level, arrived, coeff_ref, weight_ref, turned):
    depth = count.bit_length() - 1
    cols, chans = arrived.shape[1], arrived.shape[2]

    def down(level, index):
        if level == 0:
            return arrived[index]
        even = down(level - 1, 2 * index)
        odd = down(level - 1, 2 * index + 1)
        coeff_ref[offset(count, level - 1) + index] = (odd - even).astype(BF16)
        return even + odd

    coeff_ref[count - 1] = down(depth, 0).astype(BF16)
    mixed, flats = [], []
    for level in range(depth + 1):
        first = offset(count, level)
        total = max(count >> (level + 1), 1)
        flat = coeff_ref[first : first + total].astype(F32).reshape(total * cols, chans).astype(BF16)
        flats.append(flat)
        mixed.append(
            apply_weight(flat, weight_ref[first_level + level], turned).reshape(total, cols, chans)
        )
    return mixed, flats


def far_back(count, mixed, leaving, cols):
    depth = count.bit_length() - 1

    def up(level, index, value):
        if level == 0:
            leaving[index, 0:cols] = value
            return
        detail = mixed[level - 1][index]
        up(level - 1, 2 * index, value - detail)
        up(level - 1, 2 * index + 1, value + detail)

    up(depth, 0, mixed[depth][0])


def swap(count, me, source, target, send, recv, step):
    peer = lax.rem(me + step, count)
    return pltpu.make_async_remote_copy(
        src_ref=source.at[peer],
        dst_ref=target.at[me],
        send_sem=send.at[step],
        recv_sem=recv.at[step],
        device_id={"gx": peer},
        device_id_type=pl.DeviceIdType.MESH,
    )


def exchange_start(count, me, source, target, send, recv):
    @pl.loop(1, count)
    def _(step):
        swap(count, me, source, target, send, recv, step).start()

    target[me] = source[me]


def exchange_wait(count, me, source, target, send, recv):
    @pl.loop(1, count)
    def _(step):
        swap(count, me, source, target, send, recv, step).wait()


def sent_wait(count, me, source, target, send, recv):
    @pl.loop(1, count)
    def _(step):
        swap(count, me, source, target, send, recv, step).wait_send()


def send_block(count, me, block, share, source, target, send, recv):
    @pl.loop(0, share)
    def _(turn):
        step = lax.rem(block * share + turn - me + count, count)

        @pl.when(step > 0)
        def _():
            swap(count, me, source, target, send, recv, step).start()


def wait_block(count, me, block, share, source, target, send, recv):
    @pl.loop(0, share)
    def _(turn):
        step = lax.rem(me - block * share - turn + count, count)

        @pl.when(step > 0)
        def _():
            swap(count, me, source, target, send, recv, step).wait_recv()


def main_kernel(
    count, depth, factors, scales, scale_all, near_cuts, far_cuts,
    fields_ref, cot_ref, raw_mix_ref, raw_point_ref, bias_ref,
    mixed_back, out_ref, mix_ref, point_ref, gbias_ref,
    weight_ref, back_weight, held, coeff, mixed_all, back_ref, far_coeff, far_scratch,
    source_a, arrived_a, leaving_a, landed_a,
    source_b, arrived_b, leaving_b, landed_b,
    near, near_sum, far, far_sum, slots_0, slots_1, slots_2, slots_3,
    load_sem, send_a, recv_a, send_b, recv_b, send_c, recv_c, send_d, recv_d,
    send_0, recv_0, send_1, recv_1, send_2, recv_2, send_3, recv_3,
):
    me = lax.axis_index("gx")
    blocks, rows, wide, chans = coeff.shape
    cols = source_a.shape[1]
    tiles = chans // 8
    share, piece = wide // cols, LANES // cols
    barrier = pltpu.get_barrier_semaphore()

    def load(source, block):
        return pltpu.make_async_copy(
            source.at[:, pl.ds(block * wide, wide), :], held.at[block], load_sem.at[block]
        )

    for block in range(blocks):
        load(fields_ref, block).start()

    @pl.loop(1, count)
    def _(step):
        pl.semaphore_signal(
            barrier,
            inc=1,
            device_id={"gx": lax.rem(me + step, count)},
            device_id_type=pl.DeviceIdType.MESH,
        )

    near[...] = jnp.zeros_like(near)
    join_weights(raw_mix_ref, raw_point_ref, scales, GELU_A, weight_ref)
    join_weights(raw_mix_ref, raw_point_ref, scales, 1.0, back_weight)

    @pl.loop(0, blocks)
    def _(block):
        load(fields_ref, block).wait()

        @pl.loop(0, wide // LANES)
        def _(sub):
            here = pl.ds(pl.multiple_of(sub * LANES, LANES), LANES)

            def tree(level, index):
                if level == 0:
                    return held[block, index, here, :].astype(F32)
                even = tree(level - 1, 2 * index)
                odd = tree(level - 1, 2 * index + 1)
                coeff[block, offset(rows, level - 1) + index, here, :] = (odd - even).astype(BF16)
                return even + odd

            source_a[pl.ds(block * share + sub * piece, piece)] = tree(depth, 0).reshape(
                piece, cols, chans
            )

        load(cot_ref, block).start()

    pl.semaphore_wait(barrier, count - 1)
    exchange_start(count, me, source_a, arrived_a, send_a, recv_a)

    @pl.loop(0, blocks)
    def _(block):
        mix_block(depth, coeff.at[block], weight_ref, mixed_all.at[block], False)

    exchange_wait(count, me, source_a, arrived_a, send_a, recv_a)
    mixed, _ = far_levels(count, depth, arrived_a, far_coeff, weight_ref, False)
    far_back(count, mixed, leaving_a, cols)
    exchange_start(count, me, leaving_a, landed_a, send_b, recv_b)

    @pl.loop(0, blocks)
    def _(block):
        load(cot_ref, block).wait()
        wait_block(count, me, block, share, leaving_a, landed_a, send_b, recv_b)

        @pl.loop(0, wide // LANES)
        def _(sub):
            here = pl.ds(pl.multiple_of(sub * LANES, LANES), LANES)

            def tree(level, index, value):
                if level == 0:
                    cot = held[block, index, here, :].astype(F32)
                    return slope_of(value, cot).astype(BF16).astype(F32)
                place = offset(rows, level - 1) + index
                detail = mixed_all[block, place, here, :]
                even = tree(level - 1, 2 * index, value - detail)
                odd = tree(level - 1, 2 * index + 1, value + detail)
                back_ref[block, place, here, :] = (odd - even).astype(BF16)
                return even + odd

            pieces = pl.ds(block * share + sub * piece, piece)
            start = landed_a[pieces].reshape(LANES, chans) + bias_ref[...].astype(F32) * GELU_A
            source_b[pieces] = tree(depth, 0, start).reshape(piece, cols, chans)

        send_block(count, me, block, share, source_b, arrived_b, send_c, recv_c)
        for level in range(depth):
            first, number = offset(rows, level), rows >> (level + 1)
            left = coeff[block, first : first + number].reshape(number * wide, chans)
            right = back_ref[block, first : first + number].reshape(number * wide, chans)
            near[level * tiles : (level + 1) * tiles] += outer(left, right).reshape(tiles, 8, chans)

    one, two = digit_orders(count)
    streams = [
        Stream(near, slots_0, near_sum, send_0, recv_0, 0, near_cuts[0], one, me),
        Stream(near, slots_1, near_sum, send_1, recv_1, near_cuts[0], near_cuts[1], two, me),
        Stream(far, slots_2, far_sum, send_2, recv_2, 0, far_cuts[0], two, me),
        Stream(far, slots_3, far_sum, send_3, recv_3, far_cuts[0], far_cuts[1], one, me),
    ]

    def step_on(pair, stage):
        for stream in pair:
            stream.finish(stage)
            stream.start(stage + 1)

    def mix_back(low, high):
        @pl.loop(low, high)
        def _(block):
            mix_block(depth, back_ref.at[block], back_weight, mixed_back.at[block], True)

    for stream in streams[:2]:
        stream.start(0)
    arrived_b[me] = source_b[me]
    mix_back(0, 1)
    step_on(streams[:2], 0)
    mix_back(1, 2)
    exchange_wait(count, me, source_b, arrived_b, send_c, recv_c)
    mixed, flats = far_levels(count, depth, arrived_b, far_scratch, back_weight, True)
    far_back(count, mixed, leaving_b, cols)
    part = jnp.sum(jnp.sum(arrived_b[...], axis=0), axis=0, keepdims=True)
    leaving_b[:, cols:] = jnp.broadcast_to(part[None], (count, leaving_b.shape[1] - cols, chans))
    exchange_start(count, me, leaving_b, landed_b, send_d, recv_d)
    for level, flat in enumerate(flats):
        first = offset(count, level)
        total = max(count >> (level + 1), 1)
        prior = far_coeff[first : first + total].astype(F32).reshape(total * cols, chans)
        far[level * tiles : (level + 1) * tiles] = outer(prior.astype(BF16), flat).reshape(
            tiles, 8, chans
        )
    for stream in streams[2:]:
        stream.start(0)
    mix_back(2, blocks)
    for stage in range(max(len(stream.stages) for stream in streams)):
        step_on(streams[:2], stage + 1)
        step_on(streams[2:], stage)
    exchange_wait(count, me, leaving_b, landed_b, send_d, recv_d)
    sent_wait(count, me, leaving_a, landed_a, send_b, recv_b)
    out_ref[...] = landed_b[:, 0:cols]
    gsum = jnp.sum(landed_b[:, cols : cols + 8], axis=0) * scale_all
    gbias_ref[...] = gsum[0:1].astype(BF16)
    point = jnp.zeros((chans, chans), F32)
    for level in range(len(scales)):
        source, base = (near_sum, level) if level < depth else (far_sum, level - depth)
        raw = source[base * tiles : (base + 1) * tiles].reshape(chans, chans) * scales[level]
        mix_ref[level] = (raw * factors[level]).astype(BF16)
        point = point + raw
    point_ref[...] = (point * scale_all).astype(BF16)


def main_call(fields, cotangent, weights, point_weight, bias, step, count, factors, scales, scale_all):
    rows, width, chans = fields.shape
    depth = rows.bit_length() - 1
    levels = weights.shape[0]
    blocks, cols = width // step, width // count
    tiles = chans // 8
    near_levels, far_count = depth, levels - depth
    cut = lambda number: ((number + 1) // 2 * tiles, number // 2 * tiles)
    near_cuts, far_cuts = cut(near_levels), cut(far_count)
    one, two = digit_orders(count)
    needs = [
        stream_needs(length, order)
        for length, order in zip(near_cuts + far_cuts, (one, two, two, one))
    ]
    near, far = near_levels * tiles, far_count * tiles
    row_shape, padded = (count, cols, chans), (count, cols + 8, chans)
    whole_shape = (blocks, rows, step, chans)
    rows_f32 = pltpu.VMEM(row_shape, F32)
    vmem = pl.BlockSpec(memory_space=pltpu.VMEM)
    hbm = pl.BlockSpec(memory_space=pltpu.HBM)
    return pl.pallas_call(
        functools.partial(main_kernel, count, depth, factors, scales, scale_all, near_cuts, far_cuts),
        in_specs=[hbm, hbm, vmem, vmem, vmem],
        out_specs=(vmem,) * 5,
        out_shape=(
            pltpu.VMEM(whole_shape, BF16),
            pltpu.VMEM(row_shape, F32),
            pltpu.VMEM(weights.shape, BF16),
            pltpu.VMEM((chans, chans), BF16),
            pltpu.VMEM((1, chans), BF16),
        ),
        scratch_shapes=[
            pltpu.VMEM(weights.shape, BF16),
            pltpu.VMEM(weights.shape, BF16),
            pltpu.VMEM(whole_shape, BF16),
            pltpu.VMEM(whole_shape, BF16),
            pltpu.VMEM(whole_shape, F32),
            pltpu.VMEM(whole_shape, BF16),
            pltpu.VMEM(row_shape, BF16),
            pltpu.VMEM(row_shape, BF16),
            rows_f32, rows_f32, rows_f32, rows_f32,
            rows_f32, rows_f32, pltpu.VMEM(padded, F32), pltpu.VMEM(padded, F32),
            pltpu.VMEM((near, 8, chans), F32),
            pltpu.VMEM((near, 8, chans), F32),
            pltpu.VMEM((far, 8, chans), F32),
            pltpu.VMEM((far, 8, chans), F32),
        ]
        + [pltpu.VMEM((place, 8, chans), F32) for place, _ in needs]
        + [pltpu.SemaphoreType.DMA((blocks,))]
        + [pltpu.SemaphoreType.DMA((count,))] * 8
        + [pltpu.SemaphoreType.DMA((sems,)) for _, sems in needs for _ in range(2)],
        compiler_params=pltpu.CompilerParams(
            collective_id=0, has_side_effects=True, vmem_limit_bytes=50 << 20,
        ),
    )(fields, cotangent, weights, point_weight, bias)


def synth_kernel(
    depth, mixed_ref, coarse_ref, mix_ref, point_ref, gbias_ref,
    out_ref, mix_out, point_out, gbias_out, held, sems,
):
    blocks, rows, wide, chans = mixed_ref.shape
    small = [
        pltpu.make_async_copy(source, target, sems.at[blocks + index])
        for index, (source, target) in enumerate(
            ((mix_ref, mix_out), (point_ref, point_out), (gbias_ref, gbias_out))
        )
    ]
    for copy in small:
        copy.start()

    def store(block):
        return pltpu.make_async_copy(
            held.at[block], out_ref.at[:, pl.ds(block * wide, wide), :], sems.at[block]
        )

    @pl.loop(0, blocks)
    def _(block):
        @pl.loop(0, wide // LANES)
        def _(sub):
            cols = pl.ds(pl.multiple_of(sub * LANES, LANES), LANES)
            there = pl.ds(pl.multiple_of(block * wide + sub * LANES, LANES), LANES)

            def tree(level, index, value):
                if level == 0:
                    held[block, index, cols, :] = value.astype(BF16)
                    return
                detail = mixed_ref[block, offset(rows, level - 1) + index, cols, :].astype(F32)
                tree(level - 1, 2 * index, value - detail)
                tree(level - 1, 2 * index + 1, value + detail)

            tree(depth, 0, coarse_ref[there, :])

        store(block).start()

    @pl.loop(0, blocks)
    def _(block):
        store(block).wait()

    for copy in small:
        copy.wait()


def shards(fields, cotangent, point_weight, mix_weight, bias_vec):
    rows, width, chans = fields.shape
    depth = rows.bit_length() - 1
    count = lax.axis_size("gx")
    levels = mix_weight.shape[0]
    step = 64
    blocks = width // step
    scales = [2.0 ** -(level + 1) for level in range(levels - 1)] + [2.0 ** -(levels - 1)]
    bias = bias_vec.reshape(1, chans)
    total_rows = rows * count
    members = [width * total_rows / 2 ** (level + 1) for level in range(levels - 1)] + [width]
    factors = [1.0 / math.sqrt(value) for value in members]
    scale_all = 1.0 / math.sqrt(total_rows * width)
    mixed, coarse, grad_mix, grad_point, grad_bias = main_call(
        fields, cotangent, mix_weight, point_weight, bias, step, count, factors, scales, scale_all,
    )

    vmem = pl.BlockSpec(memory_space=pltpu.VMEM)
    hbm = pl.BlockSpec(memory_space=pltpu.HBM)
    grad_input, grad_mix, grad_point, grad_bias = pl.pallas_call(
        functools.partial(synth_kernel, depth),
        in_specs=[vmem] * 5,
        out_specs=(hbm,) * 4,
        out_shape=(
            jax.ShapeDtypeStruct(fields.shape, BF16),
            jax.ShapeDtypeStruct(mix_weight.shape, BF16),
            jax.ShapeDtypeStruct(point_weight.shape, BF16),
            jax.ShapeDtypeStruct((1, chans), BF16),
        ),
        scratch_shapes=[
            pltpu.VMEM((blocks, rows, step, chans), BF16),
            pltpu.SemaphoreType.DMA((blocks + 3,)),
        ],
        compiler_params=pltpu.CompilerParams(vmem_limit_bytes=24 << 20),
    )(mixed, coarse.reshape(width, chans), grad_mix, grad_point, grad_bias)
    return (grad_input, grad_mix, grad_point, grad_bias.reshape(chans))


def solution(mesh):
    in_specs = (P("gx", "ga", None), P("gx", "ga", None), P(), P(), P())
    out_specs = (P("gx", "ga", None), P("ga", None, None), P("ga", None), P("ga"))
    return jax.shard_map(shards, mesh=mesh, in_specs=in_specs, out_specs=out_specs, check_vma=False)
```

```python
import functools
import math

import jax
import jax.numpy as jnp
from jax import lax
from jax.experimental import pallas as pl
from jax.experimental.pallas import tpu as pltpu
from jax.sharding import PartitionSpec as P

F32 = jnp.float32
BF16 = jnp.bfloat16
LANES = 16
GELU_K = math.sqrt(2.0 / math.pi)
GELU_C = 0.044715
GELU_A = (GELU_K * GELU_C) ** (1.0 / 3.0)
GELU_B = GELU_K / GELU_A


def offset(rows, level):
    return rows - (rows >> level)


def outer(left, right):
    return lax.dot_general(left, right, (((0,), (0,)), ((), ())), preferred_element_type=F32)


def apply_weight(rows, weight, turned):
    sides = (((1,), (1 if turned else 0,)), ((), ()))
    return lax.dot_general(rows, weight, sides, preferred_element_type=F32)


def slope_of(value, cot):
    square = value * value
    bend = jnp.tanh(value * (GELU_B + square))
    ramp = value * (0.5 * GELU_B + 1.5 * square)
    return ((1.0 + bend) * (0.5 + (1.0 - bend) * ramp)).astype(BF16) * cot


def join_weights(mix_ref, point_ref, scales, factor, joined):
    point = point_ref[...].astype(F32)
    for level, scale in enumerate(scales):
        joined[level] = ((mix_ref[level].astype(F32) + point) * (scale * factor)).astype(BF16)


def mix_block(depth, coeff_ref, weight_ref, mixed_ref, turned):
    rows = 1 << depth
    wide = coeff_ref.shape[1]
    for level in range(depth):
        first, count = offset(rows, level), rows >> (level + 1)
        flat = coeff_ref[first : first + count].reshape(count * wide, coeff_ref.shape[2])
        mixed_ref[first : first + count] = (
            apply_weight(flat, weight_ref[level], turned)
            .reshape(count, wide, weight_ref.shape[2])
            .astype(mixed_ref.dtype)
        )


class Stream:
    def __init__(self, total, slots, result, send, recv, part, digits, me):
        self.total, self.slots, self.result = total, slots, result
        self.send, self.recv = send, recv
        self.room = slots
        (start, length), place = part, 0
        scatter = []
        for stride, radix in digits:
            mine = lax.rem(me // stride, radix)
            split = length % radix == 0
            size = length // radix if split else length
            keep = start + mine * size if split else start
            plan = []
            for turn in range(1, radix):
                other = lax.rem(mine + turn, radix)
                give = start + other * size if split else start
                plan.append((me + (other - mine) * stride, give, place + (turn - 1) * size))
            scatter.append(("sum", plan, split, size, keep))
            start, length, place = keep, size, place + (radix - 1) * size
        self.stages = scatter[:]
        for kind, plan, split, size, keep in scatter[::-1]:
            if split:
                again = [(peer, keep, keep) for peer, _, _ in plan]
                self.stages.append(("spread", again, split, size, keep))
        self.last = len(scatter) - 1

    def copies(self, index):
        kind, plan, split, size, keep = self.stages[index]
        source = self.total if kind == "sum" else self.result
        target = self.slots if kind == "sum" else self.result
        return [
            pltpu.make_async_remote_copy(
                src_ref=source.at[pl.ds(give, size)],
                dst_ref=target.at[pl.ds(place, size)],
                send_sem=self.send.at[index],
                recv_sem=self.recv.at[index],
                device_id={"gx": peer},
                device_id_type=pl.DeviceIdType.MESH,
            )
            for peer, give, place in plan
        ]

    def start(self, index):
        if index < len(self.stages):
            for copy in self.copies(index):
                copy.start()

    def finish(self, index):
        if index >= len(self.stages):
            return
        kind, plan, split, size, keep = self.stages[index]
        wait_rows(self.room, len(plan) * size, self.recv.at[index])
        wait_rows(self.room, len(plan) * size, self.send.at[index])
        if kind == "sum":
            here = pl.ds(keep, size)
            into = self.result if index == self.last else self.total
            value = self.total[here]
            for _, _, place in plan:
                value = value + self.slots[pl.ds(place, size)]
            into[here] = value


def stream_needs(length, digits):
    place, stages = 0, 0
    for stride, radix in digits:
        split = length % radix == 0
        size = length // radix if split else length
        place, stages = place + (radix - 1) * size, stages + (2 if split else 1)
        length = size
    return place, stages


def digit_orders(count):
    bits = count.bit_length() - 2
    plan, stride = [(1, 2)], 2
    while bits > 0:
        size = 1 if bits % 2 else 2
        plan.append((stride, 1 << size))
        stride, bits = stride << size, bits - size
    wide = [(2, count // 2)] if 2 < count <= 32 else plan[1:]
    return plan, plan[:1] + plan[2:] + plan[1:2], plan[:1] + wide


def far_coeffs(count, arrived, coeff_ref):
    depth = count.bit_length() - 1

    def down(level, index):
        if level == 0:
            return arrived[index]
        even = down(level - 1, 2 * index)
        odd = down(level - 1, 2 * index + 1)
        coeff_ref[offset(count, level - 1) + index] = (odd - even).astype(BF16)
        return even + odd

    coeff_ref[count - 1] = down(depth, 0).astype(BF16)


def far_flat(count, level, coeff_ref):
    first, total = offset(count, level), max(count >> (level + 1), 1)
    cols, chans = coeff_ref.shape[1:]
    return coeff_ref[first : first + total].astype(F32).reshape(total * cols, chans).astype(BF16)


def far_mix(count, first_level, coeff_ref, weight_ref, turned):
    cols, chans = coeff_ref.shape[1:]
    return [
        apply_weight(far_flat(count, level, coeff_ref), weight_ref[first_level + level], turned).reshape(
            max(count >> (level + 1), 1), cols, chans
        )
        for level in range(count.bit_length())
    ]


def far_back(count, mixed, leaving, cols):
    depth = count.bit_length() - 1

    def up(level, index, value):
        if level == 0:
            leaving[index, 0:cols] = value
            return
        detail = mixed[level - 1][index]
        up(level - 1, 2 * index, value - detail)
        up(level - 1, 2 * index + 1, value + detail)

    up(depth, 0, mixed[depth][0])


def swap(count, me, source, target, send, recv, step):
    peer = lax.rem(me + step, count)
    return pltpu.make_async_remote_copy(
        src_ref=source.at[peer],
        dst_ref=target.at[me],
        send_sem=send,
        recv_sem=recv,
        device_id={"gx": peer},
        device_id_type=pl.DeviceIdType.MESH,
    )


def exchange_start(count, me, source, target, send, recv):
    @pl.loop(1, count)
    def _(step):
        swap(count, me, source, target, send, recv, step).start()

    target[me] = source[me]


def wait_rows(buffer, number, sem):
    rows = buffer.at[pl.ds(0, number)]
    pltpu.make_async_copy(rows, rows, sem).wait()


def send_block(count, me, block, share, source, target, send, recv):
    @pl.loop(0, share)
    def _(turn):
        step = lax.rem(block * share + turn - me + count, count)

        @pl.when(step > 0)
        def _():
            swap(count, me, source, target, send, recv, step).start()


def wait_block(me, block, share, target, recv):
    own = me // share

    @pl.when(own == block)
    def _():
        if share > 1:
            wait_rows(target, share - 1, recv.at[block])

    @pl.when(own != block)
    def _():
        wait_rows(target, share, recv.at[block])


def main_kernel(
    count, depth, factors, scales, scale_all, near_cuts, plans,
    fields_ref, cot_ref, raw_mix_ref, raw_point_ref, bias_ref,
    mixed_back, out_ref, mix_ref, point_ref, gbias_ref,
    mix_held, point_held, bias_held, weight_ref, back_weight, held, coeff, mixed_all, back_ref, far_coeff, far_scratch,
    source_a, arrived_a, leaving_a, landed_a,
    source_b, arrived_b, leaving_b, landed_b,
    near, near_sum, far, far_sum, slots_0, slots_1, slots_2, slots_3,
    load_sem, weight_sem, send_a, recv_a, send_b, recv_b, send_c, recv_c, send_d, recv_d,
    send_0, recv_0, send_1, recv_1, send_2, recv_2, send_3, recv_3,
):
    me = lax.axis_index("gx")
    blocks, rows, wide, chans = coeff.shape
    cols = source_a.shape[1]
    tiles = chans // 8
    share, piece = wide // cols, LANES // cols
    barrier = pltpu.get_barrier_semaphore()

    def load(source, block):
        return pltpu.make_async_copy(
            source.at[:, pl.ds(block * wide, wide), :], held.at[block], load_sem.at[block]
        )

    @pl.loop(1, count)
    def _(step):
        pl.semaphore_signal(
            barrier,
            inc=1,
            device_id={"gx": lax.rem(me + step, count)},
            device_id_type=pl.DeviceIdType.MESH,
        )

    weights = [
        pltpu.make_async_copy(source, target, weight_sem.at[index])
        for index, (source, target) in enumerate(
            ((raw_mix_ref, mix_held), (raw_point_ref, point_held), (bias_ref, bias_held))
        )
    ]
    for copy in weights:
        copy.start()
    for block in range(blocks):
        load(fields_ref, block).start()
    near[...] = jnp.zeros_like(near)
    for copy in weights:
        copy.wait()
    join_weights(mix_held, point_held, scales, GELU_A, weight_ref)
    join_weights(mix_held, point_held, scales, 1.0, back_weight)

    @pl.loop(0, blocks)
    def _(block):
        load(fields_ref, block).wait()

        @pl.loop(0, wide // LANES)
        def _(sub):
            here = pl.ds(pl.multiple_of(sub * LANES, LANES), LANES)

            def tree(level, index):
                if level == 0:
                    return held[block, index, here, :].astype(F32)
                even = tree(level - 1, 2 * index)
                odd = tree(level - 1, 2 * index + 1)
                coeff[block, offset(rows, level - 1) + index, here, :] = (odd - even).astype(BF16)
                return even + odd

            source_a[pl.ds(block * share + sub * piece, piece)] = tree(depth, 0).reshape(
                piece, cols, chans
            )

        load(cot_ref, block).start()

    def mix_out(low, high):
        @pl.loop(low, high)
        def _(block):
            mix_block(depth, coeff.at[block], weight_ref, mixed_all.at[block], False)

    pl.semaphore_wait(barrier, count - 1)
    exchange_start(count, me, source_a, arrived_a, send_a.at[0], recv_a.at[0])
    mix_out(0, blocks)
    wait_rows(arrived_a, count - 1, recv_a.at[0])
    wait_rows(source_a, count - 1, send_a.at[0])
    far_coeffs(count, arrived_a, far_coeff)
    mixed = far_mix(count, depth, far_coeff, weight_ref, False)
    far_back(count, mixed, leaving_a, cols)
    exchange_start(count, me, leaving_a, landed_a, send_b.at[0], recv_b.at[me // share])

    @pl.loop(0, blocks)
    def _(block):
        load(cot_ref, block).wait()
        wait_block(me, block, share, landed_a, recv_b)

        @pl.loop(0, wide // LANES)
        def _(sub):
            here = pl.ds(pl.multiple_of(sub * LANES, LANES), LANES)

            def tree(level, index, value):
                if level == 0:
                    return slope_of(value, held[block, index, here, :])
                place = offset(rows, level - 1) + index
                detail = mixed_all[block, place, here, :]
                even = tree(level - 1, 2 * index, value - detail)
                odd = tree(level - 1, 2 * index + 1, value + detail)
                back_ref[block, place, here, :] = (odd - even).astype(BF16)
                return (even + odd).astype(F32)

            pieces = pl.ds(block * share + sub * piece, piece)
            start = landed_a[pieces].reshape(LANES, chans) + bias_held[...].astype(F32) * GELU_A
            source_b[pieces] = tree(depth, 0, start).reshape(piece, cols, chans)

        send_block(count, me, block, share, source_b, arrived_b, send_c.at[0], recv_c.at[0])

    def near_outer(levels):
        @pl.loop(0, blocks)
        def _(block):
            for level in levels:
                first, number = offset(rows, level), rows >> (level + 1)
                left = coeff[block, first : first + number].reshape(number * wide, chans)
                right = back_ref[block, first : first + number].reshape(number * wide, chans)
                near[level * tiles : (level + 1) * tiles] += outer(left, right).reshape(
                    tiles, 8, chans
                )

    def mix_back(low, high):
        @pl.loop(low, high)
        def _(block):
            mix_block(depth, back_ref.at[block], back_weight, mixed_back.at[block], True)

    streams = [
        Stream(near, slots_0, near_sum, send_0, recv_0, near_cuts[0], plans[0], me),
        Stream(near, slots_1, near_sum, send_1, recv_1, near_cuts[1], plans[1], me),
        Stream(near, slots_2, near_sum, send_2, recv_2, near_cuts[2], plans[2], me),
        Stream(far, slots_3, far_sum, send_3, recv_3, (0, far.shape[0]), plans[3], me),
    ]

    def begin(which):
        streams[which].start(0)

    def step_on(which, stage):
        streams[which].finish(stage)
        streams[which].start(stage + 1)

    groups = [range(low // tiles, (low + size) // tiles) for low, size in near_cuts]
    near_outer(groups[0])
    begin(0)
    near_outer(groups[1])
    begin(1)
    step_on(0, 0)
    near_outer(groups[2])
    begin(2)
    step_on(1, 0)
    arrived_b[me] = source_b[me]
    wait_rows(arrived_b, count - 1, recv_c.at[0])
    far_coeffs(count, arrived_b, far_scratch)
    for level in range(count.bit_length()):
        far[level * tiles : (level + 1) * tiles] = outer(
            far_flat(count, level, far_coeff), far_flat(count, level, far_scratch)
        ).reshape(tiles, 8, chans)
    begin(3)
    step_on(2, 0)
    mixed = far_mix(count, depth, far_scratch, back_weight, True)
    far_back(count, mixed, leaving_b, cols)
    part = jnp.sum(jnp.sum(arrived_b[...], axis=0), axis=0, keepdims=True)
    leaving_b[:, cols:] = jnp.broadcast_to(part[None], (count, leaving_b.shape[1] - cols, chans))
    step_on(0, 1)
    step_on(3, 0)
    step_on(1, 1)
    exchange_start(count, me, leaving_b, landed_b, send_d.at[0], recv_d.at[0])
    mix_back(0, blocks // 2)
    wait_rows(source_b, count - 1, send_c.at[0])
    wait_rows(leaving_a, count - 1, send_b.at[0])
    order = [(2, 1), (0, 2), (1, 2), (0, 3), (3, 1), (2, 2), (1, 3), (2, 3)]
    for which, stage in order[:3]:
        step_on(which, stage)
    mix_back(blocks // 2, blocks)
    for which, stage in order[3:]:
        step_on(which, stage)
    for stage in range(4, max(len(stream.stages) for stream in streams)):
        for which in (2, 0, 1):
            step_on(which, stage)
    for stage in range(2, len(streams[3].stages)):
        step_on(3, stage)
    wait_rows(leaving_b, count - 1, send_d.at[0])
    wait_rows(landed_b, count - 1, recv_d.at[0])
    out_ref[...] = landed_b[:, 0:cols]
    gsum = jnp.sum(landed_b[:, cols : cols + 8], axis=0) * scale_all
    gbias_ref[...] = gsum[0:1].astype(BF16)
    point = jnp.zeros((chans, chans), F32)
    for level in range(len(scales)):
        source, base = (near_sum, level) if level < depth else (far_sum, level - depth)
        raw = source[base * tiles : (base + 1) * tiles].reshape(chans, chans) * scales[level]
        mix_ref[level] = (raw * factors[level]).astype(BF16)
        point = point + raw
    point_ref[...] = (point * scale_all).astype(BF16)


def main_call(fields, cotangent, weights, point_weight, bias, step, count, factors, scales, scale_all):
    rows, width, chans = fields.shape
    depth = rows.bit_length() - 1
    levels = weights.shape[0]
    blocks, cols = width // step, width // count
    tiles = chans // 8
    near, far = depth * tiles, (levels - depth) * tiles
    middle = (depth + 1) // 2
    near_cuts = [
        (low * tiles, (high - low) * tiles) for low, high in ((middle, depth), (1, middle), (0, 1))
    ]
    one, two, three = digit_orders(count)
    plans = [two, one, three, three]
    needs = [
        stream_needs(length, plan)
        for length, plan in zip([size for _, size in near_cuts] + [far], plans)
    ]
    row_shape, padded = (count, cols, chans), (count, cols + 8, chans)
    whole_shape = (blocks, rows, step, chans)
    rows_f32 = pltpu.VMEM(row_shape, F32)
    vmem = pl.BlockSpec(memory_space=pltpu.VMEM)
    hbm = pl.BlockSpec(memory_space=pltpu.HBM)
    return pl.pallas_call(
        functools.partial(main_kernel, count, depth, factors, scales, scale_all, near_cuts, plans),
        in_specs=[hbm] * 5,
        out_specs=(vmem,) * 5,
        out_shape=(
            pltpu.VMEM(whole_shape, BF16),
            pltpu.VMEM(row_shape, F32),
            pltpu.VMEM(weights.shape, BF16),
            pltpu.VMEM((chans, chans), BF16),
            pltpu.VMEM((1, chans), BF16),
        ),
        scratch_shapes=[
            pltpu.VMEM(weights.shape, BF16),
            pltpu.VMEM(point_weight.shape, BF16),
            pltpu.VMEM(bias.shape, BF16),
            pltpu.VMEM(weights.shape, BF16),
            pltpu.VMEM(weights.shape, BF16),
            pltpu.VMEM(whole_shape, BF16),
            pltpu.VMEM(whole_shape, BF16),
            pltpu.VMEM(whole_shape, F32),
            pltpu.VMEM(whole_shape, BF16),
            pltpu.VMEM(row_shape, BF16),
            pltpu.VMEM(row_shape, BF16),
            rows_f32, rows_f32, rows_f32, rows_f32,
            rows_f32, rows_f32, pltpu.VMEM(padded, F32), pltpu.VMEM(padded, F32),
            pltpu.VMEM((near, 8, chans), F32),
            pltpu.VMEM((near, 8, chans), F32),
            pltpu.VMEM((far, 8, chans), F32),
            pltpu.VMEM((far, 8, chans), F32),
        ]
        + [pltpu.VMEM((place, 8, chans), F32) for place, _ in needs]
        + [pltpu.SemaphoreType.DMA((blocks,)), pltpu.SemaphoreType.DMA((3,))]
        + [pltpu.SemaphoreType.DMA((max(blocks, 1),))] * 8
        + [pltpu.SemaphoreType.DMA((sems,)) for _, sems in needs for _ in range(2)],
        compiler_params=pltpu.CompilerParams(
            collective_id=0, has_side_effects=True, vmem_limit_bytes=50 << 20,
        ),
    )(fields, cotangent, weights, point_weight, bias)


def synth_kernel(
    depth, mixed_ref, coarse_ref, mix_ref, point_ref, gbias_ref,
    out_ref, mix_out, point_out, gbias_out, held, sems,
):
    blocks, rows, wide, chans = mixed_ref.shape
    small = [
        pltpu.make_async_copy(source, target, sems.at[held.shape[0] + index])
        for index, (source, target) in enumerate(
            ((mix_ref, mix_out), (point_ref, point_out), (gbias_ref, gbias_out))
        )
    ]
    for copy in small:
        copy.start()

    parts, thin = held.shape[0], held.shape[2]
    every = wide // thin

    def store(index):
        return pltpu.make_async_copy(
            held.at[index], out_ref.at[:, pl.ds(index * thin, thin), :], sems.at[index]
        )

    @pl.loop(0, parts)
    def _(index_out):
        block, base = index_out // every, lax.rem(index_out, every) * thin

        @pl.loop(0, thin // LANES)
        def _(sub):
            cols = pl.ds(pl.multiple_of(sub * LANES, LANES), LANES)
            inside = pl.ds(pl.multiple_of(base + sub * LANES, LANES), LANES)
            there = pl.ds(pl.multiple_of(index_out * thin + sub * LANES, LANES), LANES)

            def tree(level, index, value):
                if level == 0:
                    held[index_out, index, cols, :] = value.astype(BF16)
                    return
                detail = mixed_ref[block, offset(rows, level - 1) + index, inside, :].astype(F32)
                tree(level - 1, 2 * index, value - detail)
                tree(level - 1, 2 * index + 1, value + detail)

            tree(depth, 0, coarse_ref[there, :])

        store(index_out).start()

    @pl.loop(0, parts)
    def _(index_out):
        store(index_out).wait()

    for copy in small:
        copy.wait()


def shards(fields, cotangent, point_weight, mix_weight, bias_vec):
    rows, width, chans = fields.shape
    depth = rows.bit_length() - 1
    count = lax.axis_size("gx")
    levels = mix_weight.shape[0]
    step, thin = 64, 32
    blocks = width // step
    scales = [2.0 ** -(level + 1) for level in range(levels - 1)] + [2.0 ** -(levels - 1)]
    bias = bias_vec.reshape(1, chans)
    total_rows = rows * count
    members = [width * total_rows / 2 ** (level + 1) for level in range(levels - 1)] + [width]
    factors = [1.0 / math.sqrt(value) for value in members]
    scale_all = 1.0 / math.sqrt(total_rows * width)
    mixed, coarse, grad_mix, grad_point, grad_bias = main_call(
        fields, cotangent, mix_weight, point_weight, bias, step, count, factors, scales, scale_all,
    )

    vmem = pl.BlockSpec(memory_space=pltpu.VMEM)
    hbm = pl.BlockSpec(memory_space=pltpu.HBM)
    grad_input, grad_mix, grad_point, grad_bias = pl.pallas_call(
        functools.partial(synth_kernel, depth),
        in_specs=[vmem] * 5,
        out_specs=(hbm,) * 4,
        out_shape=(
            jax.ShapeDtypeStruct(fields.shape, BF16),
            jax.ShapeDtypeStruct(mix_weight.shape, BF16),
            jax.ShapeDtypeStruct(point_weight.shape, BF16),
            jax.ShapeDtypeStruct((1, chans), BF16),
        ),
        scratch_shapes=[
            pltpu.VMEM((width // thin, rows, thin, chans), BF16),
            pltpu.SemaphoreType.DMA((width // thin + 3,)),
        ],
        compiler_params=pltpu.CompilerParams(vmem_limit_bytes=24 << 20),
    )(mixed, coarse.reshape(width, chans), grad_mix, grad_point, grad_bias)
    return (grad_input, grad_mix, grad_point, grad_bias.reshape(chans))


def solution(mesh):
    in_specs = (P("gx", "ga", None), P("gx", "ga", None), P(), P(), P())
    out_specs = (P("gx", "ga", None), P("ga", None, None), P("ga", None), P("ga"))
    return jax.shard_map(shards, mesh=mesh, in_specs=in_specs, out_specs=out_specs, check_vma=False)
```

```python
import functools
import math

import jax
import jax.numpy as jnp
from jax import lax
from jax.experimental import pallas as pl
from jax.experimental.pallas import tpu as pltpu
from jax.sharding import PartitionSpec as P

F32 = jnp.float32
BF16 = jnp.bfloat16
LANES = 16
TAIL = (
    ("outer", 0),
    ("begin", 0),
    ("outer", 1),
    ("begin", 1),
    ("step", 0, 0),
    ("sums",),
    ("begin", 3),
    ("step", 1, 0),
    ("leave",),
    ("outer", 2),
    ("begin", 2),
    ("step", 3, 0),
    ("step", 2, 0),
    ("mix", 0),
    ("step", 0, 1),
    ("step", 1, 1),
    ("step", 3, 1),
    ("step", 2, 1),
    ("mix", 1),
    ("send",),
)
GELU_K = math.sqrt(2.0 / math.pi)
GELU_C = 0.044715
GELU_A = (GELU_K * GELU_C) ** (1.0 / 3.0)
GELU_B = GELU_K / GELU_A


def offset(rows, level):
    return rows - (rows >> level)


def outer(left, right):
    return lax.dot_general(left, right, (((0,), (0,)), ((), ())), preferred_element_type=F32)


def apply_weight(rows, weight, turned):
    sides = (((1,), (1 if turned else 0,)), ((), ()))
    return lax.dot_general(rows, weight, sides, preferred_element_type=F32)


def slope_of(value, cot):
    bend = jnp.tanh(value * (GELU_B + value * value))
    short = value.astype(BF16)
    ramp = short * (BF16(0.5 * GELU_B) + BF16(1.5) * (short * short))
    above, below = (1.0 + bend).astype(BF16), (1.0 - bend).astype(BF16)
    return above * (BF16(0.5) + below * ramp) * cot


def join_weights(mix_ref, point_ref, scales, factor, joined):
    point = point_ref[...].astype(F32)
    for level, scale in enumerate(scales):
        joined[level] = ((mix_ref[level].astype(F32) + point) * (scale * factor)).astype(BF16)


def mix_block(depth, coeff_ref, weight_ref, mixed_ref, turned):
    rows = 1 << depth
    wide = coeff_ref.shape[1]
    for level in range(depth):
        first, count = offset(rows, level), rows >> (level + 1)
        flat = coeff_ref[first : first + count].reshape(count * wide, coeff_ref.shape[2])
        mixed_ref[first : first + count] = (
            apply_weight(flat, weight_ref[level], turned)
            .reshape(count, wide, weight_ref.shape[2])
            .astype(mixed_ref.dtype)
        )


class Stream:
    def __init__(self, total, slots, result, send, recv, part, digits, me):
        self.total, self.slots, self.result = total, slots, result
        self.send, self.recv = send, recv
        self.room = slots
        (start, length), place = part, 0
        scatter = []
        for stride, radix in digits:
            mine = lax.rem(me // stride, radix)
            split = length % radix == 0
            size = length // radix if split else length
            keep = start + mine * size if split else start
            plan = []
            for turn in range(1, radix):
                other = lax.rem(mine + turn, radix)
                give = start + other * size if split else start
                plan.append((me + (other - mine) * stride, give, place + (turn - 1) * size))
            scatter.append(("sum", plan, split, size, keep))
            start, length, place = keep, size, place + (radix - 1) * size
        self.stages = scatter[:]
        for kind, plan, split, size, keep in scatter[::-1]:
            if split:
                again = [(peer, keep, keep) for peer, _, _ in plan]
                self.stages.append(("spread", again, split, size, keep))
        self.last = len(scatter) - 1

    def copies(self, index):
        kind, plan, split, size, keep = self.stages[index]
        source = self.total if kind == "sum" else self.result
        target = self.slots if kind == "sum" else self.result
        return [
            pltpu.make_async_remote_copy(
                src_ref=source.at[pl.ds(give, size)],
                dst_ref=target.at[pl.ds(place, size)],
                send_sem=self.send.at[index],
                recv_sem=self.recv.at[index],
                device_id={"gx": peer},
                device_id_type=pl.DeviceIdType.MESH,
            )
            for peer, give, place in plan
        ]

    def start(self, index):
        if index < len(self.stages):
            for copy in self.copies(index):
                copy.start()

    def finish(self, index):
        if index >= len(self.stages):
            return
        kind, plan, split, size, keep = self.stages[index]
        wait_rows(self.room, len(plan) * size, self.recv.at[index])
        wait_rows(self.room, len(plan) * size, self.send.at[index])
        if kind == "sum":
            here = pl.ds(keep, size)
            into = self.result if index == self.last else self.total
            value = self.total[here]
            for _, _, place in plan:
                value = value + self.slots[pl.ds(place, size)]
            into[here] = value


def stream_needs(length, digits):
    place, stages = 0, 0
    for stride, radix in digits:
        split = length % radix == 0
        size = length // radix if split else length
        place, stages = place + (radix - 1) * size, stages + (2 if split else 1)
        length = size
    return place, stages


def digit_orders(count):
    bits = count.bit_length() - 2
    plan, stride = [(1, 2)], 2
    while bits > 0:
        size = 1 if bits % 2 else 2
        plan.append((stride, 1 << size))
        stride, bits = stride << size, bits - size
    wide = [(2, count // 2)] if 2 < count <= 32 else plan[1:]
    return plan, plan[:1] + plan[2:] + plan[1:2], plan[:1] + wide


def far_coeffs(count, arrived, coeff_ref):
    depth = count.bit_length() - 1

    def down(level, index):
        if level == 0:
            return arrived[index]
        even = down(level - 1, 2 * index)
        odd = down(level - 1, 2 * index + 1)
        coeff_ref[offset(count, level - 1) + index] = (odd - even).astype(BF16)
        return even + odd

    coeff_ref[count - 1] = down(depth, 0).astype(BF16)


def far_flat(count, level, coeff_ref):
    first, total = offset(count, level), max(count >> (level + 1), 1)
    cols, chans = coeff_ref.shape[1:]
    return coeff_ref[first : first + total].astype(F32).reshape(total * cols, chans).astype(BF16)


def far_mix(count, first_level, coeff_ref, weight_ref, turned):
    cols, chans = coeff_ref.shape[1:]
    return [
        apply_weight(far_flat(count, level, coeff_ref), weight_ref[first_level + level], turned).reshape(
            max(count >> (level + 1), 1), cols, chans
        )
        for level in range(count.bit_length())
    ]


def far_back(count, mixed, leaving, cols):
    depth = count.bit_length() - 1

    def up(level, index, value):
        if level == 0:
            leaving[index, 0:cols] = value
            return
        detail = mixed[level - 1][index]
        up(level - 1, 2 * index, value - detail)
        up(level - 1, 2 * index + 1, value + detail)

    up(depth, 0, mixed[depth][0])


def swap(count, me, source, target, send, recv, step):
    peer = lax.rem(me + step, count)
    return pltpu.make_async_remote_copy(
        src_ref=source.at[peer],
        dst_ref=target.at[me],
        send_sem=send,
        recv_sem=recv,
        device_id={"gx": peer},
        device_id_type=pl.DeviceIdType.MESH,
    )


def exchange_start(count, me, source, target, send, recv):
    @pl.loop(1, count)
    def _(step):
        swap(count, me, source, target, send, recv, step).start()

    target[me] = source[me]


def wait_rows(buffer, number, sem):
    rows = buffer.at[pl.ds(0, number)]
    pltpu.make_async_copy(rows, rows, sem).wait()


def send_block(count, me, block, share, source, target, send, recv):
    @pl.loop(0, share)
    def _(turn):
        step = lax.rem(block * share + turn - me + count, count)

        @pl.when(step > 0)
        def _():
            swap(count, me, source, target, send, recv, step).start()


def wait_block(me, block, share, target, recv):
    own = me // share

    @pl.when(own == block)
    def _():
        if share > 1:
            wait_rows(target, share - 1, recv.at[block])

    @pl.when(own != block)
    def _():
        wait_rows(target, share, recv.at[block])


def main_kernel(
    count, depth, factors, scales, scale_all, groups, plans,
    fields_ref, cot_ref, raw_mix_ref, raw_point_ref, bias_ref,
    mixed_back, out_ref, mix_ref, point_ref, gbias_ref,
    mix_held, point_held, bias_held, weight_ref, back_weight, held, coeff, mixed_all, back_ref, far_coeff, far_scratch,
    source_a, arrived_a, leaving_a, landed_a,
    source_b, arrived_b, leaving_b, landed_b,
    grads, sums, load_sem, weight_sem, send_a, recv_a, send_b, recv_b, send_c, recv_c, send_d, recv_d,
    *rest,
):
    me = lax.axis_index("gx")
    blocks, rows, wide, chans = coeff.shape
    cols = source_a.shape[1]
    tiles = chans // 8
    share, piece = wide // cols, LANES // cols
    barrier = pltpu.get_barrier_semaphore()

    def load(source, block):
        return pltpu.make_async_copy(
            source.at[:, pl.ds(block * wide, wide), :], held.at[block], load_sem.at[block]
        )

    @pl.loop(1, count)
    def _(step):
        pl.semaphore_signal(
            barrier,
            inc=1,
            device_id={"gx": lax.rem(me + step, count)},
            device_id_type=pl.DeviceIdType.MESH,
        )

    weights = [
        pltpu.make_async_copy(source, target, weight_sem.at[index])
        for index, (source, target) in enumerate(
            ((raw_mix_ref, mix_held), (raw_point_ref, point_held), (bias_ref, bias_held))
        )
    ]
    for copy in weights:
        copy.start()
    for block in range(blocks):
        load(fields_ref, block).start()
    grads[...] = jnp.zeros_like(grads)
    for copy in weights:
        copy.wait()
    join_weights(mix_held, point_held, scales, GELU_A, weight_ref)
    join_weights(mix_held, point_held, scales, 1.0, back_weight)

    def analyse(block):
        load(fields_ref, block).wait()

        @pl.loop(0, wide // LANES)
        def _(sub):
            here = pl.ds(pl.multiple_of(sub * LANES, LANES), LANES)

            def tree(level, index):
                if level == 0:
                    return held[block, index, here, :].astype(F32)
                even = tree(level - 1, 2 * index)
                odd = tree(level - 1, 2 * index + 1)
                coeff[block, offset(rows, level - 1) + index, here, :] = (odd - even).astype(BF16)
                return even + odd

            source_a[pl.ds(block * share + sub * piece, piece)] = tree(depth, 0).reshape(
                piece, cols, chans
            )

        load(cot_ref, block).start()

    pl.loop(0, blocks - 1)(analyse)
    pl.semaphore_wait(barrier, count - 1)

    @pl.loop(0, blocks - 1)
    def _(block):
        send_block(count, me, block, share, source_a, arrived_a, send_a.at[0], recv_a.at[0])

    analyse(blocks - 1)
    send_block(count, me, blocks - 1, share, source_a, arrived_a, send_a.at[0], recv_a.at[0])
    arrived_a[me] = source_a[me]

    def mix_out(low, high):
        @pl.loop(low, high)
        def _(block):
            mix_block(depth, coeff.at[block], weight_ref, mixed_all.at[block], False)

    mix_out(0, blocks)
    wait_rows(arrived_a, count - 1, recv_a.at[0])
    wait_rows(source_a, count - 1, send_a.at[0])
    far_coeffs(count, arrived_a, far_coeff)
    mixed = far_mix(count, depth, far_coeff, weight_ref, False)
    far_back(count, mixed, leaving_a, cols)
    exchange_start(count, me, leaving_a, landed_a, send_b.at[0], recv_b.at[me // share])

    @pl.loop(0, blocks)
    def _(block):
        load(cot_ref, block).wait()
        wait_block(me, block, share, landed_a, recv_b)

        @pl.loop(0, wide // LANES)
        def _(sub):
            here = pl.ds(pl.multiple_of(sub * LANES, LANES), LANES)

            def tree(level, index, value):
                if level == 0:
                    return slope_of(value, held[block, index, here, :])
                place = offset(rows, level - 1) + index
                detail = mixed_all[block, place, here, :]
                even = tree(level - 1, 2 * index, value - detail)
                odd = tree(level - 1, 2 * index + 1, value + detail)
                back_ref[block, place, here, :] = (odd - even).astype(BF16)
                return (even + odd).astype(F32)

            pieces = pl.ds(block * share + sub * piece, piece)
            start = landed_a[pieces].reshape(LANES, chans) + bias_held[...].astype(F32) * GELU_A
            source_b[pieces] = tree(depth, 0, start).reshape(piece, cols, chans)

        send_block(count, me, block, share, source_b, arrived_b, send_c.at[0], recv_c.at[0])

    def near_outer(levels):
        @pl.loop(0, blocks)
        def _(block):
            for level in levels:
                first, number = offset(rows, level), rows >> (level + 1)
                left = coeff[block, first : first + number].reshape(number * wide, chans)
                right = back_ref[block, first : first + number].reshape(number * wide, chans)
                grads[level * tiles : (level + 1) * tiles] += outer(left, right).reshape(
                    tiles, 8, chans
                )

    def mix_back(low, high):
        @pl.loop(low, high)
        def _(block):
            mix_block(depth, back_ref.at[block], back_weight, mixed_back.at[block], True)

    number = len(groups)
    streams = [
        Stream(
            grads, rest[index], sums, rest[number + 2 * index], rest[number + 2 * index + 1],
            (low * tiles, (high - low) * tiles), plan, me,
        )
        for index, ((low, high), plan) in enumerate(zip(groups, plans))
    ]

    def begin(which):
        streams[which].start(0)

    def step_on(which, stage):
        streams[which].finish(stage)
        streams[which].start(stage + 1)

    def far_sums():
        arrived_b[me] = source_b[me]
        wait_rows(arrived_b, count - 1, recv_c.at[0])
        far_coeffs(count, arrived_b, far_scratch)
        for level in range(count.bit_length()):
            place = (depth + level) * tiles
            grads[place : place + tiles] = outer(
                far_flat(count, level, far_coeff), far_flat(count, level, far_scratch)
            ).reshape(tiles, 8, chans)

    def far_leave():
        mixed = far_mix(count, depth, far_scratch, back_weight, True)
        far_back(count, mixed, leaving_b, cols)
        part = jnp.sum(jnp.sum(arrived_b[...], axis=0), axis=0, keepdims=True)
        leaving_b[:, cols:] = jnp.broadcast_to(
            part[None], (count, leaving_b.shape[1] - cols, chans)
        )

    def far_send():
        exchange_start(count, me, leaving_b, landed_b, send_d.at[0], recv_d.at[0])

    half = blocks // 2
    actions = {
        "outer": lambda which: near_outer(range(*groups[which])),
        "begin": begin,
        "step": step_on,
        "sums": far_sums,
        "leave": far_leave,
        "send": far_send,
        "mix": lambda part: mix_back(part * half, half + part * (blocks - half)),
    }
    done = [-1] * len(streams)
    for action, *values in TAIL:
        actions[action](*values)
        if action == "step":
            done[values[0]] = values[1]
    for stage in range(max(len(stream.stages) for stream in streams)):
        for which, stream in enumerate(streams):
            if done[which] < stage < len(stream.stages):
                step_on(which, stage)
    wait_rows(source_b, count - 1, send_c.at[0])
    wait_rows(leaving_a, count - 1, send_b.at[0])
    wait_rows(leaving_b, count - 1, send_d.at[0])
    wait_rows(landed_b, count - 1, recv_d.at[0])
    out_ref[...] = landed_b[:, 0:cols]
    gsum = jnp.sum(landed_b[:, cols : cols + 8], axis=0) * scale_all
    gbias_ref[...] = gsum[0:1].astype(BF16)
    point = jnp.zeros((chans, chans), F32)
    for level in range(len(scales)):
        raw = sums[level * tiles : (level + 1) * tiles].reshape(chans, chans) * scales[level]
        mix_ref[level] = (raw * factors[level]).astype(BF16)
        point = point + raw
    point_ref[...] = (point * scale_all).astype(BF16)


def main_call(fields, cotangent, weights, point_weight, bias, step, count, factors, scales, scale_all):
    rows, width, chans = fields.shape
    depth = rows.bit_length() - 1
    levels = weights.shape[0]
    blocks, cols = width // step, width // count
    tiles = chans // 8
    one, two, three = digit_orders(count)
    middle = (depth + 1) // 2
    groups = [(middle, depth), (1, middle), (0, 1), (depth, levels)]
    plans = [three, three, three, three]
    needs = [stream_needs((high - low) * tiles, plan) for (low, high), plan in zip(groups, plans)]
    row_shape, padded = (count, cols, chans), (count, cols + 8, chans)
    whole_shape = (blocks, rows, step, chans)
    rows_f32 = pltpu.VMEM(row_shape, F32)
    vmem = pl.BlockSpec(memory_space=pltpu.VMEM)
    hbm = pl.BlockSpec(memory_space=pltpu.HBM)
    return pl.pallas_call(
        functools.partial(main_kernel, count, depth, factors, scales, scale_all, groups, plans),
        in_specs=[hbm] * 5,
        out_specs=(vmem,) * 5,
        out_shape=(
            pltpu.VMEM(whole_shape, BF16),
            pltpu.VMEM(row_shape, F32),
            pltpu.VMEM(weights.shape, BF16),
            pltpu.VMEM((chans, chans), BF16),
            pltpu.VMEM((1, chans), BF16),
        ),
        scratch_shapes=[
            pltpu.VMEM(weights.shape, BF16),
            pltpu.VMEM(point_weight.shape, BF16),
            pltpu.VMEM(bias.shape, BF16),
            pltpu.VMEM(weights.shape, BF16),
            pltpu.VMEM(weights.shape, BF16),
            pltpu.VMEM(whole_shape, BF16),
            pltpu.VMEM(whole_shape, BF16),
            pltpu.VMEM(whole_shape, F32),
            pltpu.VMEM(whole_shape, BF16),
            pltpu.VMEM(row_shape, BF16),
            pltpu.VMEM(row_shape, BF16),
            rows_f32, rows_f32, rows_f32, rows_f32,
            rows_f32, rows_f32, pltpu.VMEM(padded, F32), pltpu.VMEM(padded, F32),
            pltpu.VMEM((levels * tiles, 8, chans), F32),
            pltpu.VMEM((levels * tiles, 8, chans), F32),
            pltpu.SemaphoreType.DMA((blocks,)),
            pltpu.SemaphoreType.DMA((3,)),
        ]
        + [pltpu.SemaphoreType.DMA((blocks,))] * 8
        + [pltpu.VMEM((place, 8, chans), F32) for place, _ in needs]
        + [pltpu.SemaphoreType.DMA((sems,)) for _, sems in needs for _ in range(2)],
        compiler_params=pltpu.CompilerParams(
            collective_id=0, has_side_effects=True, vmem_limit_bytes=50 << 20,
        ),
    )(fields, cotangent, weights, point_weight, bias)


def synth_kernel(
    depth, mixed_ref, coarse_ref, mix_ref, point_ref, gbias_ref,
    out_ref, mix_out, point_out, gbias_out, held, sems,
):
    blocks, rows, wide, chans = mixed_ref.shape
    small = [
        pltpu.make_async_copy(source, target, sems.at[held.shape[0] + index])
        for index, (source, target) in enumerate(
            ((mix_ref, mix_out), (point_ref, point_out), (gbias_ref, gbias_out))
        )
    ]
    for copy in small:
        copy.start()

    parts, thin = held.shape[0], held.shape[2]
    every = wide // thin

    def store(index):
        return pltpu.make_async_copy(
            held.at[index], out_ref.at[:, pl.ds(index * thin, thin), :], sems.at[index]
        )

    @pl.loop(0, parts)
    def _(index_out):
        block, base = index_out // every, lax.rem(index_out, every) * thin

        @pl.loop(0, thin // LANES)
        def _(sub):
            cols = pl.ds(pl.multiple_of(sub * LANES, LANES), LANES)
            inside = pl.ds(pl.multiple_of(base + sub * LANES, LANES), LANES)
            there = pl.ds(pl.multiple_of(index_out * thin + sub * LANES, LANES), LANES)

            def tree(level, index, value):
                if level == 0:
                    held[index_out, index, cols, :] = value.astype(BF16)
                    return
                detail = mixed_ref[block, offset(rows, level - 1) + index, inside, :].astype(F32)
                tree(level - 1, 2 * index, value - detail)
                tree(level - 1, 2 * index + 1, value + detail)

            tree(depth, 0, coarse_ref[there, :])

        store(index_out).start()

    @pl.loop(0, parts)
    def _(index_out):
        store(index_out).wait()

    for copy in small:
        copy.wait()


def shards(fields, cotangent, point_weight, mix_weight, bias_vec):
    rows, width, chans = fields.shape
    depth = rows.bit_length() - 1
    count = lax.axis_size("gx")
    levels = mix_weight.shape[0]
    step, thin = 64, 32
    blocks = width // step
    scales = [2.0 ** -(level + 1) for level in range(levels - 1)] + [2.0 ** -(levels - 1)]
    bias = bias_vec.reshape(1, chans)
    total_rows = rows * count
    members = [width * total_rows / 2 ** (level + 1) for level in range(levels - 1)] + [width]
    factors = [1.0 / math.sqrt(value) for value in members]
    scale_all = 1.0 / math.sqrt(total_rows * width)
    mixed, coarse, grad_mix, grad_point, grad_bias = main_call(
        fields, cotangent, mix_weight, point_weight, bias, step, count, factors, scales, scale_all,
    )

    vmem = pl.BlockSpec(memory_space=pltpu.VMEM)
    hbm = pl.BlockSpec(memory_space=pltpu.HBM)
    grad_input, grad_mix, grad_point, grad_bias = pl.pallas_call(
        functools.partial(synth_kernel, depth),
        in_specs=[vmem] * 5,
        out_specs=(hbm,) * 4,
        out_shape=(
            jax.ShapeDtypeStruct(fields.shape, BF16),
            jax.ShapeDtypeStruct(mix_weight.shape, BF16),
            jax.ShapeDtypeStruct(point_weight.shape, BF16),
            jax.ShapeDtypeStruct((1, chans), BF16),
        ),
        scratch_shapes=[
            pltpu.VMEM((width // thin, rows, thin, chans), BF16),
            pltpu.SemaphoreType.DMA((width // thin + 3,)),
        ],
        compiler_params=pltpu.CompilerParams(vmem_limit_bytes=24 << 20),
    )(mixed, coarse.reshape(width, chans), grad_mix, grad_point, grad_bias)
    return (grad_input, grad_mix, grad_point, grad_bias.reshape(chans))


def solution(mesh):
    in_specs = (P("gx", "ga", None), P("gx", "ga", None), P(), P(), P())
    out_specs = (P("gx", "ga", None), P("ga", None, None), P("ga", None), P("ga"))
    return jax.shard_map(shards, mesh=mesh, in_specs=in_specs, out_specs=out_specs, check_vma=False)
```

```python
import functools
import math

import jax
import jax.numpy as jnp
from jax import lax
from jax.experimental import pallas as pl
from jax.experimental.pallas import tpu as pltpu
from jax.sharding import PartitionSpec as P

F32 = jnp.float32
BF16 = jnp.bfloat16
LANES = 16
TAIL = (
    ("outer", 0),
    ("begin", 0),
    ("outer", 1),
    ("begin", 1),
    ("step", 0, 0),
    ("sums",),
    ("begin", 3),
    ("step", 1, 0),
    ("leave",),
    ("outer", 2),
    ("begin", 2),
    ("step", 3, 0),
    ("step", 2, 0),
    ("step", 0, 1),
    ("step", 1, 1),
    ("step", 3, 1),
    ("step", 2, 1),
    ("send",),
    ("mix", 0),
    ("mix", 1),
)
GELU_K = math.sqrt(2.0 / math.pi)
GELU_C = 0.044715
GELU_A = (GELU_K * GELU_C) ** (1.0 / 3.0)
GELU_B = GELU_K / GELU_A


def offset(rows, level):
    return rows - (rows >> level)


def outer(left, right):
    return lax.dot_general(left, right, (((0,), (0,)), ((), ())), preferred_element_type=F32)


def apply_weight(rows, weight, turned):
    sides = (((1,), (1 if turned else 0,)), ((), ()))
    return lax.dot_general(rows, weight, sides, preferred_element_type=F32)


def slope_of(value, cot):
    bend = jnp.tanh(value * (GELU_B + value * value))
    short = value.astype(BF16)
    ramp = short * (BF16(0.5 * GELU_B) + BF16(1.5) * (short * short))
    above, below = (1.0 + bend).astype(BF16), (1.0 - bend).astype(BF16)
    return above * (BF16(0.5) + below * ramp) * cot


def join_weights(mix_ref, point_ref, scales, factor, joined):
    point = point_ref[...].astype(F32)
    for level, scale in enumerate(scales):
        joined[level] = ((mix_ref[level].astype(F32) + point) * (scale * factor)).astype(BF16)


def mix_block(depth, coeff_ref, weight_ref, mixed_ref, turned):
    rows = 1 << depth
    wide = coeff_ref.shape[1]
    for level in range(depth):
        first, count = offset(rows, level), rows >> (level + 1)
        flat = coeff_ref[first : first + count].reshape(count * wide, coeff_ref.shape[2])
        mixed_ref[first : first + count] = (
            apply_weight(flat, weight_ref[level], turned)
            .reshape(count, wide, weight_ref.shape[2])
            .astype(mixed_ref.dtype)
        )


class Stream:
    def __init__(self, total, slots, result, send, recv, part, digits, me):
        self.total, self.slots, self.result = total, slots, result
        self.send, self.recv = send, recv
        self.room = slots
        (start, length), place = part, 0
        scatter = []
        for stride, radix in digits:
            mine = lax.rem(me // stride, radix)
            split = length % radix == 0
            size = length // radix if split else length
            keep = start + mine * size if split else start
            plan = []
            for turn in range(1, radix):
                other = lax.rem(mine + turn, radix)
                give = start + other * size if split else start
                plan.append((me + (other - mine) * stride, give, place + (turn - 1) * size))
            scatter.append(("sum", plan, split, size, keep))
            start, length, place = keep, size, place + (radix - 1) * size
        self.stages = scatter[:]
        for kind, plan, split, size, keep in scatter[::-1]:
            if split:
                again = [(peer, keep, keep) for peer, _, _ in plan]
                self.stages.append(("spread", again, split, size, keep))
        self.last = len(scatter) - 1

    def copies(self, index):
        kind, plan, split, size, keep = self.stages[index]
        source = self.total if kind == "sum" else self.result
        target = self.slots if kind == "sum" else self.result
        return [
            pltpu.make_async_remote_copy(
                src_ref=source.at[pl.ds(give, size)],
                dst_ref=target.at[pl.ds(place, size)],
                send_sem=self.send.at[index],
                recv_sem=self.recv.at[index],
                device_id={"gx": peer},
                device_id_type=pl.DeviceIdType.MESH,
            )
            for peer, give, place in plan
        ]

    def start(self, index):
        if index < len(self.stages):
            for copy in self.copies(index):
                copy.start()

    def finish(self, index):
        if index >= len(self.stages):
            return
        kind, plan, split, size, keep = self.stages[index]
        wait_rows(self.room, len(plan) * size, self.recv.at[index])
        wait_rows(self.room, len(plan) * size, self.send.at[index])
        if kind == "sum":
            here = pl.ds(keep, size)
            into = self.result if index == self.last else self.total
            value = self.total[here]
            for _, _, place in plan:
                value = value + self.slots[pl.ds(place, size)]
            into[here] = value


def stream_needs(length, digits):
    place, stages = 0, 0
    for stride, radix in digits:
        split = length % radix == 0
        size = length // radix if split else length
        place, stages = place + (radix - 1) * size, stages + (2 if split else 1)
        length = size
    return place, stages


def digit_orders(count):
    bits = count.bit_length() - 2
    plan, stride = [(1, 2)], 2
    while bits > 0:
        size = 1 if bits % 2 else 2
        plan.append((stride, 1 << size))
        stride, bits = stride << size, bits - size
    wide = [(2, count // 2)] if 2 < count <= 32 else plan[1:]
    return plan, plan[:1] + plan[2:] + plan[1:2], plan[:1] + wide


def far_coeffs(count, arrived, coeff_ref):
    depth = count.bit_length() - 1

    def down(level, index):
        if level == 0:
            return arrived[index]
        even = down(level - 1, 2 * index)
        odd = down(level - 1, 2 * index + 1)
        coeff_ref[offset(count, level - 1) + index] = (odd - even).astype(BF16)
        return even + odd

    coeff_ref[count - 1] = down(depth, 0).astype(BF16)


def far_flat(count, level, coeff_ref):
    first, total = offset(count, level), max(count >> (level + 1), 1)
    cols, chans = coeff_ref.shape[1:]
    return coeff_ref[first : first + total].astype(F32).reshape(total * cols, chans).astype(BF16)


def far_mix(count, first_level, coeff_ref, weight_ref, turned):
    cols, chans = coeff_ref.shape[1:]
    return [
        apply_weight(far_flat(count, level, coeff_ref), weight_ref[first_level + level], turned).reshape(
            max(count >> (level + 1), 1), cols, chans
        )
        for level in range(count.bit_length())
    ]


def far_back(count, mixed, leaving, cols):
    depth = count.bit_length() - 1

    def up(level, index, value):
        if level == 0:
            leaving[index, 0:cols] = value
            return
        detail = mixed[level - 1][index]
        up(level - 1, 2 * index, value - detail)
        up(level - 1, 2 * index + 1, value + detail)

    up(depth, 0, mixed[depth][0])


def swap(count, me, source, target, send, recv, step):
    peer = lax.rem(me + step, count)
    return pltpu.make_async_remote_copy(
        src_ref=source.at[peer],
        dst_ref=target.at[me],
        send_sem=send,
        recv_sem=recv,
        device_id={"gx": peer},
        device_id_type=pl.DeviceIdType.MESH,
    )


def exchange_start(count, me, source, target, send, recv):
    @pl.loop(1, count)
    def _(step):
        swap(count, me, source, target, send, recv, step).start()

    target[me] = source[me]


def wait_rows(buffer, number, sem):
    rows = buffer.at[pl.ds(0, number)]
    pltpu.make_async_copy(rows, rows, sem).wait()


def send_block(count, me, block, share, source, target, send, recv):
    @pl.loop(0, share)
    def _(turn):
        step = lax.rem(block * share + turn - me + count, count)

        @pl.when(step > 0)
        def _():
            swap(count, me, source, target, send, recv, step).start()


def wait_block(me, block, share, target, recv):
    own = me // share

    @pl.when(own == block)
    def _():
        if share > 1:
            wait_rows(target, share - 1, recv.at[block])

    @pl.when(own != block)
    def _():
        wait_rows(target, share, recv.at[block])


def main_kernel(
    count, depth, factors, scales, scale_all, groups, plans,
    fields_ref, cot_ref, raw_mix_ref, raw_point_ref, bias_ref,
    mixed_back, out_ref, mix_ref, point_ref, gbias_ref,
    mix_held, point_held, bias_held, weight_ref, back_weight, held, coeff, mixed_all, back_ref, far_coeff, far_scratch,
    source_a, arrived_a, leaving_a, landed_a,
    source_b, arrived_b, leaving_b, landed_b,
    grads, sums, load_sem, weight_sem, send_a, recv_a, send_b, recv_b, send_c, recv_c, send_d, recv_d,
    *rest,
):
    me = lax.axis_index("gx")
    blocks, rows, wide, chans = coeff.shape
    cols = source_a.shape[1]
    tiles = chans // 8
    share, piece = wide // cols, LANES // cols
    barrier = pltpu.get_barrier_semaphore()

    def load(source, block):
        return pltpu.make_async_copy(
            source.at[:, pl.ds(block * wide, wide), :], held.at[block], load_sem.at[block]
        )

    @pl.loop(1, count)
    def _(step):
        pl.semaphore_signal(
            barrier,
            inc=1,
            device_id={"gx": lax.rem(me + step, count)},
            device_id_type=pl.DeviceIdType.MESH,
        )

    weights = [
        pltpu.make_async_copy(source, target, weight_sem.at[index])
        for index, (source, target) in enumerate(
            ((raw_mix_ref, mix_held), (raw_point_ref, point_held), (bias_ref, bias_held))
        )
    ]
    for copy in weights:
        copy.start()
    for block in range(blocks):
        load(fields_ref, block).start()
    grads[...] = jnp.zeros_like(grads)
    for copy in weights:
        copy.wait()
    join_weights(mix_held, point_held, scales, GELU_A, weight_ref)

    def analyse(block):
        load(fields_ref, block).wait()

        @pl.loop(0, wide // LANES)
        def _(sub):
            here = pl.ds(pl.multiple_of(sub * LANES, LANES), LANES)

            def tree(level, index):
                if level == 0:
                    return held[block, index, here, :].astype(F32)
                even = tree(level - 1, 2 * index)
                odd = tree(level - 1, 2 * index + 1)
                coeff[block, offset(rows, level - 1) + index, here, :] = (odd - even).astype(BF16)
                return even + odd

            source_a[pl.ds(block * share + sub * piece, piece)] = tree(depth, 0).reshape(
                piece, cols, chans
            )

        load(cot_ref, block).start()

    pl.loop(0, blocks - 1)(analyse)
    pl.semaphore_wait(barrier, count - 1)

    @pl.loop(0, blocks - 1)
    def _(block):
        send_block(count, me, block, share, source_a, arrived_a, send_a.at[0], recv_a.at[0])

    analyse(blocks - 1)
    send_block(count, me, blocks - 1, share, source_a, arrived_a, send_a.at[0], recv_a.at[0])
    arrived_a[me] = source_a[me]

    def mix_out(low, high):
        @pl.loop(low, high)
        def _(block):
            mix_block(depth, coeff.at[block], weight_ref, mixed_all.at[block], False)

    mix_out(0, blocks)
    join_weights(mix_held, point_held, scales, 1.0, back_weight)
    wait_rows(arrived_a, count - 1, recv_a.at[0])
    wait_rows(source_a, count - 1, send_a.at[0])
    far_coeffs(count, arrived_a, far_coeff)
    mixed = far_mix(count, depth, far_coeff, weight_ref, False)
    far_back(count, mixed, leaving_a, cols)
    exchange_start(count, me, leaving_a, landed_a, send_b.at[0], recv_b.at[me // share])

    @pl.loop(0, blocks)
    def _(block):
        load(cot_ref, block).wait()
        wait_block(me, block, share, landed_a, recv_b)

        @pl.loop(0, wide // LANES)
        def _(sub):
            here = pl.ds(pl.multiple_of(sub * LANES, LANES), LANES)

            def tree(level, index, value):
                if level == 0:
                    return slope_of(value, held[block, index, here, :])
                place = offset(rows, level - 1) + index
                detail = mixed_all[block, place, here, :]
                even = tree(level - 1, 2 * index, value - detail)
                odd = tree(level - 1, 2 * index + 1, value + detail)
                back_ref[block, place, here, :] = (odd - even).astype(BF16)
                return (even + odd).astype(F32)

            pieces = pl.ds(block * share + sub * piece, piece)
            start = landed_a[pieces].reshape(LANES, chans) + bias_held[...].astype(F32) * GELU_A
            source_b[pieces] = tree(depth, 0, start).reshape(piece, cols, chans)

        send_block(count, me, block, share, source_b, arrived_b, send_c.at[0], recv_c.at[0])

    def near_outer(levels):
        @pl.loop(0, blocks)
        def _(block):
            for level in levels:
                first, number = offset(rows, level), rows >> (level + 1)
                left = coeff[block, first : first + number].reshape(number * wide, chans)
                right = back_ref[block, first : first + number].reshape(number * wide, chans)
                grads[level * tiles : (level + 1) * tiles] += outer(left, right).reshape(
                    tiles, 8, chans
                )

    def mix_back(low, high):
        @pl.loop(low, high)
        def _(block):
            mix_block(depth, back_ref.at[block], back_weight, mixed_back.at[block], True)

    number = len(groups)
    streams = [
        Stream(
            grads, rest[index], sums, rest[number + 2 * index], rest[number + 2 * index + 1],
            (low * tiles, (high - low) * tiles), plan, me,
        )
        for index, ((low, high), plan) in enumerate(zip(groups, plans))
    ]

    def begin(which):
        streams[which].start(0)

    def step_on(which, stage):
        streams[which].finish(stage)
        streams[which].start(stage + 1)

    def far_sums():
        arrived_b[me] = source_b[me]
        wait_rows(arrived_b, count - 1, recv_c.at[0])
        far_coeffs(count, arrived_b, far_scratch)
        for level in range(count.bit_length()):
            place = (depth + level) * tiles
            grads[place : place + tiles] = outer(
                far_flat(count, level, far_coeff), far_flat(count, level, far_scratch)
            ).reshape(tiles, 8, chans)

    def far_leave():
        mixed = far_mix(count, depth, far_scratch, back_weight, True)
        far_back(count, mixed, leaving_b, cols)
        part = jnp.sum(jnp.sum(arrived_b[...], axis=0), axis=0, keepdims=True)
        leaving_b[:, cols:] = jnp.broadcast_to(
            part[None], (count, leaving_b.shape[1] - cols, chans)
        )

    def far_send():
        exchange_start(count, me, leaving_b, landed_b, send_d.at[0], recv_d.at[0])

    half = blocks // 2
    actions = {
        "outer": lambda which: near_outer(range(*groups[which])),
        "begin": begin,
        "step": step_on,
        "sums": far_sums,
        "leave": far_leave,
        "send": far_send,
        "mix": lambda part: mix_back(part * half, half + part * (blocks - half)),
    }
    done = [-1] * len(streams)
    for action, *values in TAIL:
        actions[action](*values)
        if action == "step":
            done[values[0]] = values[1]
    for stage in range(max(len(stream.stages) for stream in streams)):
        for which, stream in enumerate(streams):
            if done[which] < stage < len(stream.stages):
                step_on(which, stage)
    wait_rows(source_b, count - 1, send_c.at[0])
    wait_rows(leaving_a, count - 1, send_b.at[0])
    wait_rows(leaving_b, count - 1, send_d.at[0])
    wait_rows(landed_b, count - 1, recv_d.at[0])
    out_ref[...] = landed_b[:, 0:cols]
    gsum = jnp.sum(landed_b[:, cols : cols + 8], axis=0) * scale_all
    gbias_ref[...] = gsum[0:1].astype(BF16)
    point = jnp.zeros((chans, chans), F32)
    for level in range(len(scales)):
        raw = sums[level * tiles : (level + 1) * tiles].reshape(chans, chans) * scales[level]
        mix_ref[level] = (raw * factors[level]).astype(BF16)
        point = point + raw
    point_ref[...] = (point * scale_all).astype(BF16)


def main_call(fields, cotangent, weights, point_weight, bias, step, count, factors, scales, scale_all):
    rows, width, chans = fields.shape
    depth = rows.bit_length() - 1
    levels = weights.shape[0]
    blocks, cols = width // step, width // count
    tiles = chans // 8
    one, two, three = digit_orders(count)
    middle = (depth + 1) // 2
    groups = [(middle, depth), (1, middle), (0, 1), (depth, levels)]
    plans = [three] * 4
    needs = [stream_needs((high - low) * tiles, plan) for (low, high), plan in zip(groups, plans)]
    row_shape, padded = (count, cols, chans), (count, cols + 8, chans)
    whole_shape = (blocks, rows, step, chans)
    rows_f32 = pltpu.VMEM(row_shape, F32)
    vmem = pl.BlockSpec(memory_space=pltpu.VMEM)
    hbm = pl.BlockSpec(memory_space=pltpu.HBM)
    return pl.pallas_call(
        functools.partial(main_kernel, count, depth, factors, scales, scale_all, groups, plans),
        in_specs=[hbm] * 5,
        out_specs=(vmem,) * 5,
        out_shape=(
            pltpu.VMEM(whole_shape, BF16),
            pltpu.VMEM(row_shape, F32),
            pltpu.VMEM(weights.shape, BF16),
            pltpu.VMEM((chans, chans), BF16),
            pltpu.VMEM((1, chans), BF16),
        ),
        scratch_shapes=[
            pltpu.VMEM(weights.shape, BF16),
            pltpu.VMEM(point_weight.shape, BF16),
            pltpu.VMEM(bias.shape, BF16),
            pltpu.VMEM(weights.shape, BF16),
            pltpu.VMEM(weights.shape, BF16),
            pltpu.VMEM(whole_shape, BF16),
            pltpu.VMEM(whole_shape, BF16),
            pltpu.VMEM(whole_shape, F32),
            pltpu.VMEM(whole_shape, BF16),
            pltpu.VMEM(row_shape, BF16),
            pltpu.VMEM(row_shape, BF16),
            rows_f32, rows_f32, rows_f32, rows_f32,
            rows_f32, rows_f32, pltpu.VMEM(padded, F32), pltpu.VMEM(padded, F32),
            pltpu.VMEM((levels * tiles, 8, chans), F32),
            pltpu.VMEM((levels * tiles, 8, chans), F32),
            pltpu.SemaphoreType.DMA((blocks,)),
            pltpu.SemaphoreType.DMA((3,)),
        ]
        + [pltpu.SemaphoreType.DMA((blocks,))] * 8
        + [pltpu.VMEM((place, 8, chans), F32) for place, _ in needs]
        + [pltpu.SemaphoreType.DMA((sems,)) for _, sems in needs for _ in range(2)],
        compiler_params=pltpu.CompilerParams(
            collective_id=0, has_side_effects=True, vmem_limit_bytes=50 << 20,
        ),
    )(fields, cotangent, weights, point_weight, bias)


def synth_kernel(
    depth, mixed_ref, coarse_ref, mix_ref, point_ref, gbias_ref,
    out_ref, mix_out, point_out, gbias_out, held, sems,
):
    blocks, rows, wide, chans = mixed_ref.shape
    small = [
        pltpu.make_async_copy(source, target, sems.at[held.shape[0] + index])
        for index, (source, target) in enumerate(
            ((mix_ref, mix_out), (point_ref, point_out), (gbias_ref, gbias_out))
        )
    ]
    for copy in small:
        copy.start()

    parts, thin = held.shape[0], held.shape[2]
    every = wide // thin

    def store(index):
        return pltpu.make_async_copy(
            held.at[index], out_ref.at[:, pl.ds(index * thin, thin), :], sems.at[index]
        )

    @pl.loop(0, parts)
    def _(index_out):
        block, base = index_out // every, lax.rem(index_out, every) * thin

        @pl.loop(0, thin // LANES)
        def _(sub):
            cols = pl.ds(pl.multiple_of(sub * LANES, LANES), LANES)
            inside = pl.ds(pl.multiple_of(base + sub * LANES, LANES), LANES)
            there = pl.ds(pl.multiple_of(index_out * thin + sub * LANES, LANES), LANES)

            def tree(level, index, value):
                if level == 0:
                    held[index_out, index, cols, :] = value.astype(BF16)
                    return
                detail = mixed_ref[block, offset(rows, level - 1) + index, inside, :].astype(F32)
                tree(level - 1, 2 * index, value - detail)
                tree(level - 1, 2 * index + 1, value + detail)

            tree(depth, 0, coarse_ref[there, :])

        store(index_out).start()

    @pl.loop(0, parts)
    def _(index_out):
        store(index_out).wait()

    for copy in small:
        copy.wait()


def shards(fields, cotangent, point_weight, mix_weight, bias_vec):
    rows, width, chans = fields.shape
    depth = rows.bit_length() - 1
    count = lax.axis_size("gx")
    levels = mix_weight.shape[0]
    step, thin = 64, 32
    blocks = width // step
    scales = [2.0 ** -(level + 1) for level in range(levels - 1)] + [2.0 ** -(levels - 1)]
    bias = bias_vec.reshape(1, chans)
    total_rows = rows * count
    members = [width * total_rows / 2 ** (level + 1) for level in range(levels - 1)] + [width]
    factors = [1.0 / math.sqrt(value) for value in members]
    scale_all = 1.0 / math.sqrt(total_rows * width)
    mixed, coarse, grad_mix, grad_point, grad_bias = main_call(
        fields, cotangent, mix_weight, point_weight, bias, step, count, factors, scales, scale_all,
    )

    vmem = pl.BlockSpec(memory_space=pltpu.VMEM)
    hbm = pl.BlockSpec(memory_space=pltpu.HBM)
    grad_input, grad_mix, grad_point, grad_bias = pl.pallas_call(
        functools.partial(synth_kernel, depth),
        in_specs=[vmem] * 5,
        out_specs=(hbm,) * 4,
        out_shape=(
            jax.ShapeDtypeStruct(fields.shape, BF16),
            jax.ShapeDtypeStruct(mix_weight.shape, BF16),
            jax.ShapeDtypeStruct(point_weight.shape, BF16),
            jax.ShapeDtypeStruct((1, chans), BF16),
        ),
        scratch_shapes=[
            pltpu.VMEM((width // thin, rows, thin, chans), BF16),
            pltpu.SemaphoreType.DMA((width // thin + 3,)),
        ],
        compiler_params=pltpu.CompilerParams(vmem_limit_bytes=24 << 20),
    )(mixed, coarse.reshape(width, chans), grad_mix, grad_point, grad_bias)
    return (grad_input, grad_mix, grad_point, grad_bias.reshape(chans))


def solution(mesh):
    in_specs = (P("gx", "ga", None), P("gx", "ga", None), P(), P(), P())
    out_specs = (P("gx", "ga", None), P("ga", None, None), P("ga", None), P("ga"))
    return jax.shard_map(shards, mesh=mesh, in_specs=in_specs, out_specs=out_specs, check_vma=False)
```

```python
import functools
import math

import jax
import jax.numpy as jnp
from jax import lax
from jax.experimental import pallas as pl
from jax.experimental.pallas import tpu as pltpu
from jax.sharding import PartitionSpec as P

F32 = jnp.float32
BF16 = jnp.bfloat16
LANES = 16
TAIL = (
    ("outer", 0),
    ("begin", 0),
    ("outer", 1),
    ("begin", 1),
    ("step", 0, 0),
    ("bias",),
    ("begin", 4),
    ("sums",),
    ("begin", 3),
    ("step", 1, 0),
    ("leave",),
    ("outer", 2),
    ("begin", 2),
    ("step", 3, 0),
    ("step", 2, 0),
    ("step", 4, 0),
    ("step", 0, 1),
    ("step", 1, 1),
    ("step", 3, 1),
    ("step", 2, 1),
    ("send",),
    ("step", 4, 1),
    ("mix", 0),
    ("step", 0, 2),
    ("step", 1, 2),
    ("mix", 1),
)
GELU_K = math.sqrt(2.0 / math.pi)
GELU_C = 0.044715
GELU_A = (GELU_K * GELU_C) ** (1.0 / 3.0)
GELU_B = GELU_K / GELU_A


def offset(rows, level):
    return rows - (rows >> level)


def outer(left, right):
    return lax.dot_general(left, right, (((0,), (0,)), ((), ())), preferred_element_type=F32)


def apply_weight(rows, weight, turned):
    sides = (((1,), (1 if turned else 0,)), ((), ()))
    return lax.dot_general(rows, weight, sides, preferred_element_type=F32)


def slope_of(value, cot):
    bend = jnp.tanh(value * (GELU_B + value * value))
    short = value.astype(BF16)
    ramp = short * (BF16(0.5 * GELU_B) + BF16(1.5) * (short * short))
    above, below = (1.0 + bend).astype(BF16), (1.0 - bend).astype(BF16)
    return above * (BF16(0.5) + below * ramp) * cot


def join_weights(mix_ref, point_ref, scales, factor, joined):
    point = point_ref[...].astype(F32)
    for level, scale in enumerate(scales):
        joined[level] = ((mix_ref[level].astype(F32) + point) * (scale * factor)).astype(BF16)


def mix_block(depth, coeff_ref, weight_ref, mixed_ref, turned):
    rows = 1 << depth
    wide = coeff_ref.shape[1]
    for level in range(depth):
        first, count = offset(rows, level), rows >> (level + 1)
        flat = coeff_ref[first : first + count].reshape(count * wide, coeff_ref.shape[2])
        mixed_ref[first : first + count] = (
            apply_weight(flat, weight_ref[level], turned)
            .reshape(count, wide, weight_ref.shape[2])
            .astype(mixed_ref.dtype)
        )


class Stream:
    def __init__(self, total, slots, result, send, recv, part, digits, back, me):
        self.total, self.slots, self.result = total, slots, result
        self.send, self.recv = send, recv
        self.room = slots
        scatter = self.lay_out(part, digits, me)
        self.stages = scatter[:]
        for kind, plan, split, size, keep in self.lay_out(part, back, me)[::-1]:
            if split:
                again = [(peer, keep, keep) for peer, _, _ in plan]
                self.stages.append(("spread", again, split, size, keep))
        self.last = len(scatter) - 1

    def lay_out(self, part, digits, me):
        (start, length), place = part, 0
        scatter = []
        for stride, radix in digits:
            mine = lax.rem(me // stride, radix)
            split = length % radix == 0
            size = length // radix if split else length
            keep = start + mine * size if split else start
            plan = []
            for turn in range(1, radix):
                other = lax.rem(mine + turn, radix)
                give = start + other * size if split else start
                plan.append((me + (other - mine) * stride, give, place + (turn - 1) * size))
            scatter.append(("sum", plan, split, size, keep))
            start, length, place = keep, size, place + (radix - 1) * size
        return scatter

    def copies(self, index):
        kind, plan, split, size, keep = self.stages[index]
        source = self.total if kind == "sum" else self.result
        target = self.slots if kind == "sum" else self.result
        return [
            pltpu.make_async_remote_copy(
                src_ref=source.at[pl.ds(give, size)],
                dst_ref=target.at[pl.ds(place, size)],
                send_sem=self.send.at[index],
                recv_sem=self.recv.at[index],
                device_id={"gx": peer},
                device_id_type=pl.DeviceIdType.MESH,
            )
            for peer, give, place in plan
        ]

    def start(self, index):
        if index < len(self.stages):
            for copy in self.copies(index):
                copy.start()

    def finish(self, index):
        if index >= len(self.stages):
            return
        kind, plan, split, size, keep = self.stages[index]
        wait_rows(self.room, len(plan) * size, self.recv.at[index])
        wait_rows(self.room, len(plan) * size, self.send.at[index])
        if kind == "sum":
            here = pl.ds(keep, size)
            into = self.result if index == self.last else self.total
            value = self.total[here]
            for _, _, place in plan:
                value = value + self.slots[pl.ds(place, size)]
            into[here] = value


def stream_needs(length, digits, back):
    place, size = 0, length
    for stride, radix in digits:
        size = size // radix if size % radix == 0 else size
        place += (radix - 1) * size
    return max(place, length), len(digits) + len(back)


def digit_orders(count):
    bits = count.bit_length() - 2
    plan, stride = [(1, 2)], 2
    while bits > 0:
        size = 1 if bits % 2 else 2
        plan.append((stride, 1 << size))
        stride, bits = stride << size, bits - size
    wide = [(2, count // 2)] if 2 < count <= 32 else plan[1:]
    return plan, plan[:1] + plan[2:] + plan[1:2], plan[:1] + wide


def far_coeffs(count, arrived, coeff_ref):
    depth = count.bit_length() - 1

    def down(level, index):
        if level == 0:
            return arrived[index]
        even = down(level - 1, 2 * index)
        odd = down(level - 1, 2 * index + 1)
        coeff_ref[offset(count, level - 1) + index] = (odd - even).astype(BF16)
        return even + odd

    coeff_ref[count - 1] = down(depth, 0).astype(BF16)


def far_flat(count, level, coeff_ref):
    first, total = offset(count, level), max(count >> (level + 1), 1)
    cols, chans = coeff_ref.shape[1:]
    return coeff_ref[first : first + total].astype(F32).reshape(total * cols, chans).astype(BF16)


def far_mix(count, first_level, coeff_ref, weight_ref, turned):
    cols, chans = coeff_ref.shape[1:]
    return [
        apply_weight(far_flat(count, level, coeff_ref), weight_ref[first_level + level], turned).reshape(
            max(count >> (level + 1), 1), cols, chans
        )
        for level in range(count.bit_length())
    ]


def far_back(count, mixed, leaving):
    depth = count.bit_length() - 1

    def up(level, index, value):
        if level == 0:
            leaving[index] = value
            return
        detail = mixed[level - 1][index]
        up(level - 1, 2 * index, value - detail)
        up(level - 1, 2 * index + 1, value + detail)

    up(depth, 0, mixed[depth][0])


def swap(count, me, source, target, send, recv, step):
    peer = lax.rem(me + step, count)
    return pltpu.make_async_remote_copy(
        src_ref=source.at[peer],
        dst_ref=target.at[me],
        send_sem=send,
        recv_sem=recv,
        device_id={"gx": peer},
        device_id_type=pl.DeviceIdType.MESH,
    )


def exchange_start(count, me, source, target, send, recv):
    @pl.loop(1, count)
    def _(step):
        swap(count, me, source, target, send, recv, step).start()

    target[me] = source[me]


def wait_rows(buffer, number, sem):
    rows = buffer.at[pl.ds(0, number)]
    pltpu.make_async_copy(rows, rows, sem).wait()


def send_block(count, me, block, share, source, target, send, recv):
    @pl.loop(0, share)
    def _(turn):
        step = lax.rem(block * share + turn - me + count, count)

        @pl.when(step > 0)
        def _():
            swap(count, me, source, target, send, recv, step).start()


def wait_block(me, block, share, target, recv):
    own = me // share

    @pl.when(own == block)
    def _():
        if share > 1:
            wait_rows(target, share - 1, recv.at[block])

    @pl.when(own != block)
    def _():
        wait_rows(target, share, recv.at[block])


def main_kernel(
    count, depth, factors, scales, scale_all, groups, plans,
    fields_ref, cot_ref, raw_mix_ref, raw_point_ref, bias_ref,
    mixed_back, out_ref, mix_ref, point_ref, gbias_ref,
    mix_held, point_held, bias_held, weight_ref, back_weight, held, coeff, mixed_all, back_ref, far_coeff, far_scratch,
    source_a, arrived_a, leaving_a, landed_a,
    source_b, arrived_b, leaving_b, landed_b,
    grads, sums, load_sem, weight_sem, send_a, recv_a, send_b, recv_b, send_c, recv_c, send_d, recv_d,
    *rest,
):
    me = lax.axis_index("gx")
    blocks, rows, wide, chans = coeff.shape
    cols = source_a.shape[1]
    tiles = chans // 8
    share, piece = wide // cols, LANES // cols
    barrier = pltpu.get_barrier_semaphore()

    def load(source, block):
        return pltpu.make_async_copy(
            source.at[:, pl.ds(block * wide, wide), :], held.at[block], load_sem.at[block]
        )

    @pl.loop(1, count)
    def _(step):
        pl.semaphore_signal(
            barrier,
            inc=1,
            device_id={"gx": lax.rem(me + step, count)},
            device_id_type=pl.DeviceIdType.MESH,
        )

    weights = [
        pltpu.make_async_copy(source, target, weight_sem.at[index])
        for index, (source, target) in enumerate(
            ((raw_mix_ref, mix_held), (raw_point_ref, point_held), (bias_ref, bias_held))
        )
    ]
    for copy in weights:
        copy.start()
    for block in range(blocks):
        load(fields_ref, block).start()
    grads[...] = jnp.zeros_like(grads)
    for copy in weights:
        copy.wait()
    join_weights(mix_held, point_held, scales, GELU_A, weight_ref)

    def analyse(block):
        load(fields_ref, block).wait()

        @pl.loop(0, wide // LANES)
        def _(sub):
            here = pl.ds(pl.multiple_of(sub * LANES, LANES), LANES)

            def tree(level, index):
                if level == 0:
                    return held[block, index, here, :]
                even = tree(level - 1, 2 * index)
                odd = tree(level - 1, 2 * index + 1)
                coeff[block, offset(rows, level - 1) + index, here, :] = (odd - even).astype(BF16)
                return even.astype(F32) + odd.astype(F32)

            source_a[pl.ds(block * share + sub * piece, piece)] = tree(depth, 0).reshape(
                piece, cols, chans
            )

        load(cot_ref, block).start()

    pl.loop(0, blocks - 1)(analyse)
    pl.semaphore_wait(barrier, count - 1)

    @pl.loop(0, blocks - 1)
    def _(block):
        send_block(count, me, block, share, source_a, arrived_a, send_a.at[0], recv_a.at[0])

    analyse(blocks - 1)
    send_block(count, me, blocks - 1, share, source_a, arrived_a, send_a.at[0], recv_a.at[0])
    arrived_a[me] = source_a[me]

    def mix_out(low, high):
        @pl.loop(low, high)
        def _(block):
            mix_block(depth, coeff.at[block], weight_ref, mixed_all.at[block], False)

    mix_out(0, blocks)
    join_weights(mix_held, point_held, scales, 1.0, back_weight)
    wait_rows(arrived_a, count - 1, recv_a.at[0])
    wait_rows(source_a, count - 1, send_a.at[0])
    far_coeffs(count, arrived_a, far_coeff)
    mixed = far_mix(count, depth, far_coeff, weight_ref, False)
    far_back(count, mixed, leaving_a)
    exchange_start(count, me, leaving_a, landed_a, send_b.at[0], recv_b.at[me // share])

    @pl.loop(0, blocks)
    def _(block):
        load(cot_ref, block).wait()
        wait_block(me, block, share, landed_a, recv_b)

        @pl.loop(0, wide // LANES)
        def _(sub):
            here = pl.ds(pl.multiple_of(sub * LANES, LANES), LANES)

            def tree(level, index, value):
                if level == 0:
                    return slope_of(value, held[block, index, here, :])
                place = offset(rows, level - 1) + index
                detail = mixed_all[block, place, here, :]
                even = tree(level - 1, 2 * index, value - detail)
                odd = tree(level - 1, 2 * index + 1, value + detail)
                back_ref[block, place, here, :] = (odd - even).astype(BF16)
                return (even + odd).astype(F32)

            pieces = pl.ds(block * share + sub * piece, piece)
            start = landed_a[pieces].reshape(LANES, chans) + bias_held[...].astype(F32) * GELU_A
            source_b[pieces] = tree(depth, 0, start).reshape(piece, cols, chans)

        send_block(count, me, block, share, source_b, arrived_b, send_c.at[0], recv_c.at[0])

    def near_outer(levels):
        @pl.loop(0, blocks)
        def _(block):
            for level in levels:
                first, number = offset(rows, level), rows >> (level + 1)
                left = coeff[block, first : first + number].reshape(number * wide, chans)
                right = back_ref[block, first : first + number].reshape(number * wide, chans)
                grads[level * tiles : (level + 1) * tiles] += outer(left, right).reshape(
                    tiles, 8, chans
                )

    def mix_back(low, high):
        @pl.loop(low, high)
        def _(block):
            mix_block(depth, back_ref.at[block], back_weight, mixed_back.at[block], True)

    number = len(groups)
    streams = [
        Stream(
            grads, rest[index], sums, rest[number + 2 * index], rest[number + 2 * index + 1],
            part, *plan, me,
        )
        for index, (part, plan) in enumerate(zip(groups, plans))
    ]

    def begin(which):
        streams[which].start(0)

    def step_on(which, stage):
        streams[which].finish(stage)
        streams[which].start(stage + 1)

    def far_sums():
        arrived_b[me] = source_b[me]
        wait_rows(arrived_b, count - 1, recv_c.at[0])
        far_coeffs(count, arrived_b, far_scratch)
        for level in range(count.bit_length()):
            place = (depth + level) * tiles
            grads[place : place + tiles] = outer(
                far_flat(count, level, far_coeff), far_flat(count, level, far_scratch)
            ).reshape(tiles, 8, chans)

    def bias_sum():
        part = jnp.sum(jnp.sum(source_b[...], axis=0), axis=0, keepdims=True)
        grads[len(scales) * tiles] = jnp.broadcast_to(part, (8, chans))

    def far_leave():
        mixed = far_mix(count, depth, far_scratch, back_weight, True)
        far_back(count, mixed, leaving_b)
    def far_send():
        exchange_start(count, me, leaving_b, landed_b, send_d.at[0], recv_d.at[0])

    half = blocks // 2
    actions = {
        "bias": bias_sum,
        "outer": lambda which: near_outer(
            range(groups[which][0] // tiles, sum(groups[which]) // tiles)
        ),
        "begin": begin,
        "step": step_on,
        "sums": far_sums,
        "leave": far_leave,
        "send": far_send,
        "mix": lambda part: mix_back(part * half, half + part * (blocks - half)),
    }
    done = [-1] * len(streams)
    for action, *values in TAIL:
        actions[action](*values)
        if action == "step":
            done[values[0]] = values[1]
    for stage in range(max(len(stream.stages) for stream in streams)):
        for which, stream in enumerate(streams):
            if done[which] < stage < len(stream.stages):
                step_on(which, stage)
    wait_rows(source_b, count - 1, send_c.at[0])
    wait_rows(leaving_a, count - 1, send_b.at[0])
    wait_rows(leaving_b, count - 1, send_d.at[0])
    wait_rows(landed_b, count - 1, recv_d.at[0])
    out_ref[...] = landed_b[...]
    gbias_ref[...] = (sums[len(scales) * tiles, 0:1] * scale_all).astype(BF16)
    point = jnp.zeros((chans, chans), F32)
    for level in range(len(scales)):
        raw = sums[level * tiles : (level + 1) * tiles].reshape(chans, chans) * scales[level]
        mix_ref[level] = (raw * factors[level]).astype(BF16)
        point = point + raw
    point_ref[...] = (point * scale_all).astype(BF16)


def main_call(fields, cotangent, weights, point_weight, bias, step, count, factors, scales, scale_all):
    rows, width, chans = fields.shape
    depth = rows.bit_length() - 1
    levels = weights.shape[0]
    blocks, cols = width // step, width // count
    tiles = chans // 8
    one, two, three = digit_orders(count)
    middle = (depth + 1) // 2
    groups = [(middle, depth), (1, middle), (0, 1), (depth, levels)]
    plans = [(three, three)]*4
    groups = [(low * tiles, (high - low) * tiles) for low, high in groups] + [(levels * tiles, 1)]
    plans = plans + [(three, three)]
    needs = [stream_needs(length, *plan) for (_, length), plan in zip(groups, plans)]
    row_shape = (count, cols, chans)
    whole_shape = (blocks, rows, step, chans)
    rows_f32 = pltpu.VMEM(row_shape, F32)
    vmem = pl.BlockSpec(memory_space=pltpu.VMEM)
    hbm = pl.BlockSpec(memory_space=pltpu.HBM)
    return pl.pallas_call(
        functools.partial(main_kernel, count, depth, factors, scales, scale_all, groups, plans),
        in_specs=[hbm] * 5,
        out_specs=(vmem,) * 5,
        out_shape=(
            pltpu.VMEM(whole_shape, BF16),
            pltpu.VMEM(row_shape, F32),
            pltpu.VMEM(weights.shape, BF16),
            pltpu.VMEM((chans, chans), BF16),
            pltpu.VMEM((1, chans), BF16),
        ),
        scratch_shapes=[
            pltpu.VMEM(weights.shape, BF16),
            pltpu.VMEM(point_weight.shape, BF16),
            pltpu.VMEM(bias.shape, BF16),
            pltpu.VMEM(weights.shape, BF16),
            pltpu.VMEM(weights.shape, BF16),
            pltpu.VMEM(whole_shape, BF16),
            pltpu.VMEM(whole_shape, BF16),
            pltpu.VMEM(whole_shape, F32),
            pltpu.VMEM(whole_shape, BF16),
            pltpu.VMEM(row_shape, BF16),
            pltpu.VMEM(row_shape, BF16),
            rows_f32, rows_f32, rows_f32, rows_f32,
            rows_f32, rows_f32, rows_f32, rows_f32,
            pltpu.VMEM((levels * tiles + 1, 8, chans), F32),
            pltpu.VMEM((levels * tiles + 1, 8, chans), F32),
            pltpu.SemaphoreType.DMA((blocks,)),
            pltpu.SemaphoreType.DMA((3,)),
        ]
        + [pltpu.SemaphoreType.DMA((blocks,))] * 8
        + [pltpu.VMEM((place, 8, chans), F32) for place, _ in needs]
        + [pltpu.SemaphoreType.DMA((sems,)) for _, sems in needs for _ in range(2)],
        compiler_params=pltpu.CompilerParams(
            collective_id=0, has_side_effects=True, vmem_limit_bytes=50 << 20,
        ),
    )(fields, cotangent, weights, point_weight, bias)


def synth_kernel(
    depth, mixed_ref, coarse_ref, mix_ref, point_ref, gbias_ref,
    out_ref, mix_out, point_out, gbias_out, held, sems,
):
    blocks, rows, wide, chans = mixed_ref.shape
    small = [
        pltpu.make_async_copy(source, target, sems.at[held.shape[0] + index])
        for index, (source, target) in enumerate(
            ((mix_ref, mix_out), (point_ref, point_out), (gbias_ref, gbias_out))
        )
    ]
    for copy in small:
        copy.start()

    parts, thin = held.shape[0], held.shape[2]
    every = wide // thin

    def store(index):
        return pltpu.make_async_copy(
            held.at[index], out_ref.at[:, pl.ds(index * thin, thin), :], sems.at[index]
        )

    @pl.loop(0, parts)
    def _(index_out):
        block, base = index_out // every, lax.rem(index_out, every) * thin

        @pl.loop(0, thin // LANES)
        def _(sub):
            cols = pl.ds(pl.multiple_of(sub * LANES, LANES), LANES)
            inside = pl.ds(pl.multiple_of(base + sub * LANES, LANES), LANES)
            there = pl.ds(pl.multiple_of(index_out * thin + sub * LANES, LANES), LANES)

            def tree(level, index, value):
                if level == 0:
                    held[index_out, index, cols, :] = value.astype(BF16)
                    return
                detail = mixed_ref[block, offset(rows, level - 1) + index, inside, :].astype(F32)
                tree(level - 1, 2 * index, value - detail)
                tree(level - 1, 2 * index + 1, value + detail)

            tree(depth, 0, coarse_ref[there, :])

        store(index_out).start()

    @pl.loop(0, parts)
    def _(index_out):
        store(index_out).wait()

    for copy in small:
        copy.wait()


def shards(fields, cotangent, point_weight, mix_weight, bias_vec):
    rows, width, chans = fields.shape
    depth = rows.bit_length() - 1
    count = lax.axis_size("gx")
    levels = mix_weight.shape[0]
    step, thin = 64, 32
    blocks = width // step
    scales = [2.0 ** -(level + 1) for level in range(levels - 1)] + [2.0 ** -(levels - 1)]
    bias = bias_vec.reshape(1, chans)
    total_rows = rows * count
    members = [width * total_rows / 2 ** (level + 1) for level in range(levels - 1)] + [width]
    factors = [1.0 / math.sqrt(value) for value in members]
    scale_all = 1.0 / math.sqrt(total_rows * width)
    mixed, coarse, grad_mix, grad_point, grad_bias = main_call(
        fields, cotangent, mix_weight, point_weight, bias, step, count, factors, scales, scale_all,
    )

    vmem = pl.BlockSpec(memory_space=pltpu.VMEM)
    hbm = pl.BlockSpec(memory_space=pltpu.HBM)
    grad_input, grad_mix, grad_point, grad_bias = pl.pallas_call(
        functools.partial(synth_kernel, depth),
        in_specs=[vmem] * 5,
        out_specs=(hbm,) * 4,
        out_shape=(
            jax.ShapeDtypeStruct(fields.shape, BF16),
            jax.ShapeDtypeStruct(mix_weight.shape, BF16),
            jax.ShapeDtypeStruct(point_weight.shape, BF16),
            jax.ShapeDtypeStruct((1, chans), BF16),
        ),
        scratch_shapes=[
            pltpu.VMEM((width // thin, rows, thin, chans), BF16),
            pltpu.SemaphoreType.DMA((width // thin + 3,)),
        ],
        compiler_params=pltpu.CompilerParams(vmem_limit_bytes=24 << 20),
    )(mixed, coarse.reshape(width, chans), grad_mix, grad_point, grad_bias)
    return (grad_input, grad_mix, grad_point, grad_bias.reshape(chans))


def solution(mesh):
    in_specs = (P("gx", "ga", None), P("gx", "ga", None), P(), P(), P())
    out_specs = (P("gx", "ga", None), P("ga", None, None), P("ga", None), P("ga"))
    return jax.shard_map(shards, mesh=mesh, in_specs=in_specs, out_specs=out_specs, check_vma=False)
```
